512 devices in a mesh: section: 2 (over y_hi), wide: 64 (over z, y_lo, core), narrow: 4 (over x).
Axes of the slice: x: 4, y: 4 (y_hi: 2, y_lo: 2; y = y_hi * 2 + y_lo), z: 16, core: 2. Of those that a mesh axis runs over, the one named last changes fastest.
Arguments:
- token_shard: int32 [16384, 1], P(('section', 'wide')), may hold values from 0 to 127; in each aligned block of 128 rows (0 to 127, 128 to 255, ...) at most 2 rows name the same one
- token_row: int32 [16384], P(('section', 'wide')), may hold values from 0 to 511
- table: bfloat16 [65536, 8192], P(('section', 'wide'), 'narrow'), may hold values from -51 to 51
- gain: float32 [8192], P('narrow'), may hold values from 0.1 to 1.9
- key_value_weight: bfloat16 [2048, 8192], P(('section', 'wide'), 'narrow'), may hold values from -0.0625 to 0.0625
- kv_target: bfloat16 [16384, 2048], P(('section', 'wide'), 'narrow'), may hold values from -6 to 6
Outputs:
- table_grad: bfloat16 [65536, 8192], P(('section', 'wide'), 'narrow')
The draws below stay inside these ranges and needn't reach their ends.
Inputs may be any that keep to these rules, and one draw needn't show every extreme that they name: `token_shard`: among the rows of one device, no value is named by more than 2 rows.
All inputs are finite; a program needn't handle non-finite values.
Results may differ from the reference program's by a relative error of at most 0.0056.
Values may be sent and summed in bfloat16 or wider, within the bound.
A program may use at most 64 MiB of HBM per device.

```python
import math
import jax
import jax.numpy as jnp
import numpy as np
from jax import lax

D = 8192
KV_WIDTH = 2048
VOCAB_DEV = 512
TOK_DEV = 128
OWNERS = 128
SLOTS = 2
VOCAB = 65536
TOKENS = 16384


def draw_table(key, part):
    row_key, jitter_key, base_key = jax.random.split(jax.random.fold_in(key, 11), 3)
    position = jnp.arange(D, dtype=jnp.float32)[None, :] / D
    jitter = jax.random.uniform(jitter_key, (1, D), jnp.float32, 0.7, 1.4)
    row_gain = jnp.exp(jax.random.uniform(row_key, (VOCAB, 1), jnp.float32, math.log(0.3), math.log(3.0)))
    column_gain = 0.3 * jnp.exp(math.log(10.0) * position) * jitter
    base = jnp.clip(jax.random.normal(base_key, (VOCAB, D), jnp.float32), -4.0, 4.0)
    return (base * row_gain * column_gain).astype(jnp.bfloat16)


def with_ends(entries, rng, low, largest):
    spot = [jax.random.randint(jax.random.fold_in(rng, axis), (), 0, length) for axis, length in enumerate(entries.shape)]
    widest = entries.shape.index(max(entries.shape))
    beside = spot[:widest] + [(spot[widest] + 1) % entries.shape[widest]] + spot[widest + 1:]
    return entries.at[tuple(spot)].set(low).at[tuple(beside)].set(largest)


def level_of(rng, extent, shards, least, largest):
    factor_of, own = 1.0, jax.random.fold_in(rng, 6)
    for axis_at, blocks in shards:
        steps = jnp.exp(jax.random.uniform(jax.random.fold_in(own, axis_at), (blocks,), jnp.float32, least / len(shards), largest / len(shards)))
        factor_of = factor_of * jnp.repeat(steps, extent[axis_at] // blocks).reshape([-1 if axis == axis_at else 1 for axis in range(len(extent))])
    return factor_of


def assign_block(stream_key, own, number, rows, amount, top, bound, lean):
    sequence = jax.random.permutation(stream_key, amount)
    heavy_load, usual = portions_of(amount, rows * top, bound, lean, True), portions_of(amount, rows * top, bound, lean, False)
    places = jnp.arange(amount)

    def named(sizes, offset_by):
        used = int((sizes > 0).sum())
        fixed = max(1, used // 4)
        shifted = fixed + (places - fixed + offset_by * (used - fixed)) % max(1, amount - fixed)
        return jnp.zeros((amount,), jnp.int32).at[sequence[jnp.where(places < fixed, places, shifted)]].set(jnp.asarray(sizes, jnp.int32))

    sizes = jnp.where(number % 4 == 0, named(heavy_load, number // 4), named(usual, number - number // 4 - 1))
    mixed = jax.random.permutation(jax.random.fold_in(own, 3), amount)
    donor, receiver = mixed[0:amount // 2 * 2:2], mixed[1:amount // 2 * 2:2]
    slack = jnp.minimum(sizes[donor] - 1, bound - sizes[receiver]) // 2
    slack = jnp.where((donor == sequence[0]) | (receiver == sequence[0]) | (sizes[receiver] == 0), 0, jnp.maximum(slack, 0))
    shifted = jax.random.randint(jax.random.fold_in(own, 4), (amount // 2,), 0, 1 << 20) % (slack + 1)
    sizes = sizes.at[donor].add(-shifted).at[receiver].add(shifted)
    items = jnp.searchsorted(jnp.cumsum(sizes), jnp.arange(rows * top), side="right").astype(jnp.int32)
    table = items.reshape(top, rows).T
    table = table[jax.random.permutation(jax.random.fold_in(own, 1), rows)]
    offset_by = jax.random.randint(jax.random.fold_in(own, 2), (rows, 1), 0, top)
    return jnp.take_along_axis(table, (jnp.arange(top)[None, :] + offset_by) % top, axis=1)


def portions_of(count, total, bound, skew, full):
    weights = [(1 << 20) // math.isqrt(standing ** skew) + 1 for standing in range(1, count + 1)]
    largest = bound if full else min(bound, max(-(-total // count), total * weights[0] // sum(weights)))
    least = 1 if total - largest >= count - 1 else 0
    counts, rest = [largest] + [least] * (count - 1), total - largest - least * (count - 1)
    while rest > 0:
        candidates = [i for i in range(1, count) if counts[i] < largest] or [i for i in range(1, count) if counts[i] < bound]
        mass, remaining = sum([weights[i] for i in candidates]), rest
        for i in candidates:
            more = min(bound - counts[i], max(1, remaining * weights[i] // mass), rest)
            counts[i] = counts[i] + more
            rest = rest - more
    return np.array(counts)


def normal_values(own_key, dims, width, reach, cuts=(), kind=jnp.bfloat16):
    result = width * jax.random.normal(own_key, dims, jnp.float32)
    if cuts:
        result = result * level_of(own_key, dims, cuts, -0.22, 0.18)
    return jnp.clip(result, -reach, reach).astype(kind)


def setup_inputs(seed: int = 0) -> dict:
    keys = jax.random.split(jax.random.key(seed), 7)
    token_shard_keys = jax.random.split(jax.random.fold_in(keys[0], 1), TOKENS // TOK_DEV)
    token_shard_turns = jax.random.permutation(jax.random.fold_in(keys[0], 3), TOKENS // TOK_DEV)
    token_shard = jax.vmap(lambda own, number: assign_block(jax.random.fold_in(keys[0], 2), own, number, TOK_DEV, OWNERS, 1, SLOTS, 1))(token_shard_keys, token_shard_turns).reshape((TOKENS, 1))
    token_row = with_ends(jax.random.randint(keys[1], (TOKENS,), 0, VOCAB_DEV), jax.random.fold_in(keys[1], 1), 0, VOCAB_DEV - 1).astype(jnp.int32)
    table = draw_table(jax.random.fold_in(keys[6], 71), 0)
    gain = jnp.clip(1.0 + 0.18 * jax.random.normal(keys[3], (D,), jnp.float32), 0.1, 1.9)
    key_value_weight = normal_values(keys[4], (KV_WIDTH, D), D ** -0.5, 0.0625, ((0, 128), (1, 4)))
    kv_target = normal_values(keys[5], (TOKENS, KV_WIDTH), 1.0, 6.0, ((0, 128), (1, 4)))
    return dict(token_shard=token_shard, token_row=token_row, table=table, gain=gain, key_value_weight=key_value_weight, kv_target=kv_target)


EPSILON = 1e-05

def reference(token_shard, token_row, table, gain, key_value_weight, kv_target):
    token_id = (token_shard[:, 0] * VOCAB_DEV + token_row).astype(jnp.int32)

    def block_pass(inputs):
        block_ids, block_target = inputs
        hidden = jnp.take(table, block_ids, axis=0)
        rows_float = hidden.astype(jnp.float32)
        mean_square = lax.optimization_barrier(jnp.sum(rows_float * rows_float, axis=1)) / D
        row_scale = lax.rsqrt(mean_square + EPSILON)
        normed = (rows_float * row_scale[:, None] * gain[None, :]).astype(jnp.bfloat16)
        projected = lax.dot_general(normed, key_value_weight, (((1,), (1,)), ((), ())), preferred_element_type=jnp.float32)
        residual = (projected - block_target.astype(jnp.float32)).astype(jnp.bfloat16)
        back_rows = jnp.dot(residual, key_value_weight, preferred_element_type=jnp.float32)
        weighted = back_rows * gain[None, :]
        inner_sum = lax.optimization_barrier(jnp.sum(weighted * rows_float, axis=1))
        grad_rows = row_scale[:, None] * weighted - rows_float * (row_scale ** 3 * inner_sum / D)[:, None]
        return grad_rows.astype(jnp.bfloat16)
    grouped = lax.map(block_pass, (token_id.reshape(-1, TOK_DEV), kv_target.reshape(-1, TOK_DEV, KV_WIDTH)))
    grad_rows = grouped.reshape(TOKENS, D)
    table_grad = jax.ops.segment_sum(grad_rows.astype(jnp.float32), token_id, num_segments=VOCAB)
    return table_grad.astype(jnp.bfloat16)
```

```python
import functools

import jax
import jax.numpy as jnp
from jax import lax
from jax.experimental import pallas as pl
from jax.experimental.pallas import tpu as pltpu
from jax.sharding import PartitionSpec as P

MESH = pl.DeviceIdType.MESH
D = 8192
EPSILON = 1e-05
NY, NZ, NC, NX = 4, 16, 2, 4
GROUP = NY * NZ * NC
SPLIT = 512
TILE = 256
IDS = 128


def kernel(
    shard_col,
    shard_row,
    row_col,
    target_ref,
    gain_ref,
    weight_hbm,
    table_hbm,
    out_ref,
    full,
    table,
    send_one,
    recv_one,
    send_two,
    recv_two,
    hidden,
    normed,
    own_part,
    part_out,
    part_in,
    resid,
    small_out,
    small_in,
    inner_out,
    inner_in,
    local_sem,
    table_sem,
    recv_a,
    recv_b,
    sent_a,
    sent_b,
    one_recv,
    one_sent,
    two_recv,
    two_sent,
    small_recv,
    small_sent,
    part_recv,
    part_sent,
    resid_recv,
    resid_sent,
    inner_recv,
    inner_sent,
):
    f32, bf16 = jnp.float32, jnp.bfloat16
    section, wide, x = lax.axis_index("section"), lax.axis_index("wide"), lax.axis_index("narrow")
    z, c = wide // 4, wide % 2
    y = section * 2 + (wide // 2) % 2
    slots = recv_two.shape[0] * recv_two.shape[1]
    tokens = target_ref.shape[0]
    depth = full.shape[1]
    width = full.shape[2]
    cols_a, cols_b = pl.ds(0, SPLIT), pl.ds(SPLIT, width - SPLIT)

    def device(yy, zz, cc, xx):
        return (yy // 2, zz * 4 + (yy % 2) * 2 + cc, xx)

    def block(yy, zz, cc):
        return (yy // 2) * (NZ * 4) + zz * 4 + (yy % 2) * 2 + cc

    def yy_of(step):
        return lax.rem(y + step + NY, NY)

    def zz_of(step):
        return lax.rem(z + step + NZ, NZ)

    def xx_of(step):
        return lax.rem(x + step + NX, NX)

    load_weight = pltpu.make_async_copy(weight_hbm, full.at[block(y, z, c)], local_sem)
    load_weight.start()
    load_table = pltpu.make_async_copy(table_hbm, table, table_sem)
    load_table.start()

    barrier = pltpu.get_barrier_semaphore()

    def greet_z(step, carry):
        pl.semaphore_signal(barrier, inc=1, device_id=device(y, zz_of(step), c, x), device_id_type=MESH)
        return carry

    lax.fori_loop(1, NZ, greet_z, 0)
    here = y * 2 + c

    def greet_y(step, carry):
        other = lax.rem(here + step, NY * NC)
        pl.semaphore_signal(barrier, inc=1, device_id=device(other // 2, z, other % 2, x), device_id_type=MESH)
        return carry

    lax.fori_loop(1, NY * NC, greet_y, 0)
    for step in range(1, NX):
        pl.semaphore_signal(barrier, inc=1, device_id=device(y, z, c, xx_of(step)), device_id_type=MESH)

    holder = shard_row[...]
    earlier = lax.broadcasted_iota(jnp.int32, (tokens, tokens), 0) < lax.broadcasted_iota(
        jnp.int32, (tokens, tokens), 1
    )
    same = jnp.logical_and(shard_col[...] == holder, earlier)
    rank = jnp.sum(jnp.where(same, 1.0, 0.0), axis=0, keepdims=True).astype(jnp.int32)
    hold_z = (holder // 4) % NZ
    hold_y = (holder // 64) * 4 + holder % 4
    slot_of = hold_z * (NY * NC * 2) + hold_y * 2 + rank
    place = jnp.where(lax.broadcasted_iota(jnp.int32, (slots, tokens), 0) == slot_of, 1.0, 0.0).astype(bf16)
    lane = lax.broadcasted_iota(jnp.int32, (tokens, IDS), 1)
    row = row_col[...]
    ids = jnp.where(lane == 0, row // 16 + 1, jnp.where(lane == 1, row % 16, 0)).astype(f32).astype(bf16)
    kept = target_ref.shape[1]
    per_z = slots // NZ
    payload = jnp.dot(place, target_ref[...], preferred_element_type=f32).astype(bf16)
    send_one[:, :, 0:kept] = payload.reshape(NZ, per_z, kept)
    payload_ids = jnp.dot(place, ids, preferred_element_type=f32).astype(bf16)
    send_one[:, :, kept:] = payload_ids.reshape(NZ, per_z, IDS)

    pl.semaphore_wait(barrier, (NZ - 1) + (NY * NC - 1) + (NX - 1))

    def copy_one(to_z, from_z):
        return pltpu.make_async_remote_copy(
            src_ref=send_one.at[to_z],
            dst_ref=recv_one.at[from_z],
            send_sem=one_sent,
            recv_sem=one_recv.at[from_z],
            device_id=device(y, to_z, c, x),
            device_id_type=MESH,
        )

    def start_one(step, carry):
        copy_one(zz_of(step), z).start()
        return carry

    lax.fori_loop(1, NZ, start_one, 0)

    def copy_weight(which, yy, zz, cc, to):
        cols, recv, sent = (cols_a, recv_a, sent_a) if which == "a" else (cols_b, recv_b, sent_b)
        piece = full.at[block(yy, zz, cc), :, cols]
        return pltpu.make_async_remote_copy(
            src_ref=piece,
            dst_ref=piece,
            send_sem=sent,
            recv_sem=recv.at[block(yy, zz, cc)],
            device_id=to,
            device_id_type=MESH,
        )

    above, below = device(yy_of(1), z, c, x), device(yy_of(-1), z, c, x)
    opposite = device(yy_of(2), z, c, x)
    after, before = device(y, zz_of(1), c, x), device(y, zz_of(-1), c, x)
    partner = device(y, z, 1 - c, x)

    def pass_on(which, yy, zz, targets):
        for to in targets:
            copy_weight(which, yy, zz, c, to).start()

    def arrive(which, yy, zz, cc):
        copy_weight(which, yy, zz, cc, partner).wait_recv()

    load_weight.wait()
    pass_on("b", y, z, (after, before, above, below, partner))
    pass_on("a", y, z, (after, before, above, below, opposite, partner))
    recv_one[z] = send_one[z]
    for step in range(1, NY):
        arrive("a", yy_of(step), z, c)
        pass_on("a", yy_of(step), z, (after, before, partner))

    def first_hand(distance, sign, ahead):
        zz = zz_of(sign * distance)
        onward = after if sign < 0 else before
        arrive("b", y, zz, c)
        if ahead is True:
            pass_on("b", y, zz, (onward,))
        elif ahead is not None:
            pl.when(ahead)(lambda: pass_on("b", y, zz, (onward,)))
        pass_on("b", y, zz, (above, below, partner))
        for step in range(NY):
            arrive("a", yy_of(step), zz, c)
            if ahead is True:
                pass_on("a", yy_of(step), zz, (onward,))
            elif ahead is not None:
                pl.when(ahead)(functools.partial(pass_on, "a", yy_of(step), zz, (onward,)))
            pass_on("a", yy_of(step), zz, (partner,))

    def second_hand(distance, sign):
        zz = zz_of(sign * distance)
        arrive("b", yy_of(-1), zz, c)
        pl.when(distance % 2 == 0)(lambda: pass_on("b", yy_of(-1), zz, (above,)))
        pass_on("b", yy_of(-1), zz, (partner,))
        arrive("b", yy_of(1), zz, c)
        pl.when(distance % 2 == 1)(lambda: pass_on("b", yy_of(1), zz, (below,)))
        pass_on("b", yy_of(1), zz, (partner,))

    def third_hand(distance, sign):
        zz = zz_of(sign * distance)
        arrive("b", yy_of(2), zz, c)
        pass_on("b", yy_of(2), zz, (partner,))

    def spread(distance, carry):
        first_hand(distance, -1, True)
        first_hand(distance, 1, distance < NZ // 2 - 1)
        second_hand(distance - 1, -1)
        pl.when(distance > 1)(lambda: second_hand(distance - 1, 1))
        pl.when(distance > 1)(lambda: third_hand(distance - 2, -1))
        pl.when(distance > 2)(lambda: third_hand(distance - 2, 1))
        return carry

    lax.fori_loop(1, 4, spread, 0)

    def wait_one(step, carry):
        copy_one(z, zz_of(step)).wait_recv()
        return carry

    lax.fori_loop(1, NZ, wait_one, 0)
    out_slot = lax.broadcasted_iota(jnp.int32, (slots, slots), 0)
    in_slot = lax.broadcasted_iota(jnp.int32, (slots, slots), 1)
    per_y = slots // (NY * NC)
    from_slot = ((out_slot % per_y) // 2) * per_z + (out_slot // per_y) * 2 + out_slot % 2
    order = jnp.where(in_slot == from_slot, 1.0, 0.0).astype(bf16)
    arrived = recv_one[...].reshape(slots, kept + IDS)
    send_two[...] = (
        jnp.dot(order, arrived, preferred_element_type=f32).astype(bf16).reshape(NY * NC, per_y, kept + IDS)
    )

    def copy_two(to_y, from_y):
        return pltpu.make_async_remote_copy(
            src_ref=send_two.at[to_y],
            dst_ref=recv_two.at[from_y],
            send_sem=two_sent,
            recv_sem=two_recv.at[from_y],
            device_id=device(to_y // 2, z, to_y % 2, x),
            device_id_type=MESH,
        )

    def start_two(step, carry):
        copy_two(lax.rem(here + step, NY * NC), here).start()
        return carry

    lax.fori_loop(1, NY * NC, start_two, 0)
    recv_two[here] = send_two[here]

    lax.fori_loop(4, 6, spread, 0)

    def wait_two(step, carry):
        copy_two(here, lax.rem(here + step, NY * NC)).wait_recv()
        return carry

    lax.fori_loop(1, NY * NC, wait_two, 0)

    load_table.wait()
    rows_here = table.shape[0]
    named = recv_two[:, :, kept:].reshape(slots, IDS).astype(f32)
    wanted = (named[:, 0:1] - 1.0) * 16.0 + named[:, 1:2]
    pick = jnp.where(
        lax.broadcasted_iota(jnp.int32, (slots, rows_here), 1).astype(f32) == wanted, 1.0, 0.0
    ).astype(bf16)
    square_sum = jnp.zeros((slots, 1), f32)
    for tile in range(width // 512):
        at = pl.ds(tile * 512, 512)
        picked = jnp.dot(pick, table[:, at], preferred_element_type=f32)
        hidden[:, at] = picked.astype(bf16)
        square_sum += jnp.sum(picked * picked, axis=1, keepdims=True)
    diagonal = out_slot == in_slot

    def as_row(column):
        return jnp.sum(jnp.where(diagonal, column, 0.0), axis=0, keepdims=True)

    def as_column(line):
        return jnp.sum(jnp.where(diagonal, line, 0.0), axis=1, keepdims=True)

    def copy_small(source, landing, sent, recv, step):
        return pltpu.make_async_remote_copy(
            src_ref=source,
            dst_ref=landing.at[step - 1],
            send_sem=sent.at[step - 1],
            recv_sem=recv.at[step - 1],
            device_id=device(y, z, c, xx_of(step)),
            device_id_type=MESH,
        )

    square_row = as_row(square_sum)
    small_out[...] = jnp.broadcast_to(square_row, small_out.shape)
    for step in range(1, NX):
        copy_small(small_out, small_in, small_sent, small_recv, step).start()

    lax.fori_loop(6, 8, spread, 0)
    half = NZ // 2
    first_hand(half, -1, None)
    for sign in (-1, 1):
        second_hand(half - 1, sign)
        third_hand(half - 2, sign)

    for step in range(1, NX):
        copy_small(small_out, small_in, small_sent, small_recv, step).wait_recv()
    total = square_row
    for step in range(1, NX):
        total += small_in[step - 1][0:1, :]
    row_scale = lax.rsqrt(as_column(total) / D + EPSILON)
    for tile in range(width // 512):
        at = pl.ds(tile * 512, 512)
        normed[:, at] = (hidden[:, at].astype(f32) * row_scale * gain_ref[:, at]).astype(bf16)

    second_hand(half, -1)
    for sign in (-1, 1):
        third_hand(half - 1, sign)
    third_hand(half, -1)

    def wait_partner(zz, carry):
        for yy in range(NY):
            arrive("a", yy, zz, 1 - c)
            arrive("b", yy, zz, 1 - c)
        return carry

    lax.fori_loop(0, NZ, wait_partner, 0)

    blocks = TILE // depth
    tiles_x = kept // TILE

    def project(tile):
        rows = full[pl.ds(tile * blocks, blocks)].reshape(TILE, width)
        return lax.dot_general(normed[...], rows, (((1,), (1,)), ((), ())), preferred_element_type=f32)

    def copy_part(step, part):
        return pltpu.make_async_remote_copy(
            src_ref=part_out.at[step - 1, part],
            dst_ref=part_in.at[step - 1, part],
            send_sem=part_sent.at[step - 1, part],
            recv_sem=part_recv.at[step - 1, part],
            device_id=device(y, z, c, xx_of(step)),
            device_id_type=MESH,
        )

    for step in (2, 1, 3):
        for part in range(tiles_x):
            part_out[step - 1, part] = project(xx_of(step) * tiles_x + part).astype(bf16)
            copy_part(step, part).start()
    for part in range(tiles_x):
        own_part[part] = project(x * tiles_x + part)

    def copy_resid(step, part):
        return pltpu.make_async_remote_copy(
            src_ref=resid.at[x, part],
            dst_ref=resid.at[x, part],
            send_sem=resid_sent.at[step - 1, part],
            recv_sem=resid_recv.at[step - 1, part],
            device_id=device(y, z, c, xx_of(step)),
            device_id_type=MESH,
        )

    inner = jnp.zeros((slots, 1), f32)
    for part in range(tiles_x):
        projected = own_part[part]
        for step in range(1, NX):
            copy_part(step, part).wait_recv()
            projected += part_in[step - 1, part].astype(f32)
        goal = recv_two[:, :, part * TILE : (part + 1) * TILE].reshape(slots, TILE)
        residual = (projected - goal.astype(f32)).astype(bf16)
        resid[x, part] = residual
        for step in (2, 1, 3):
            copy_resid(step, part).start()
        inner += jnp.sum(projected * residual.astype(f32), axis=1, keepdims=True)
    inner_row = as_row(inner)
    inner_out[...] = jnp.broadcast_to(inner_row, inner_out.shape)
    for step in range(1, NX):
        copy_small(inner_out, inner_in, inner_sent, inner_recv, step).start()

    def landed(step, part):
        return pltpu.make_async_remote_copy(
            src_ref=resid.at[xx_of(-step), part],
            dst_ref=resid.at[xx_of(-step), part],
            send_sem=resid_sent.at[step - 1, part],
            recv_sem=resid_recv.at[step - 1, part],
            device_id=device(y, z, c, xx_of(step)),
            device_id_type=MESH,
        )

    for step in range(1, NX):
        for part in range(tiles_x):
            landed(step, part).wait_recv()
    for step in range(1, NX):
        copy_small(inner_out, inner_in, inner_sent, inner_recv, step).wait_recv()
    inner_all = inner_row
    for step in range(1, NX):
        inner_all += inner_in[step - 1][0:1, :]
    pull = row_scale * row_scale * as_column(inner_all) / D
    wanted_row = as_row(wanted)
    put = jnp.where(
        lax.broadcasted_iota(jnp.int32, (rows_here, slots), 0).astype(f32) == wanted_row, 1.0, 0.0
    ).astype(bf16)

    def finish(tile, carry):
        at = pl.ds(pl.multiple_of(tile * TILE, TILE), TILE)
        back = jnp.zeros((slots, TILE), f32)
        for index in range(NX * tiles_x):
            rows = full[pl.ds(index * blocks, blocks), :, at].reshape(TILE, TILE)
            back += jnp.dot(resid[index // tiles_x, index % tiles_x], rows, preferred_element_type=f32)
        weighted = back * gain_ref[:, at]
        grad = (row_scale * weighted - hidden[:, at].astype(f32) * pull).astype(bf16)
        out_ref[:, at] = jnp.dot(put, grad, preferred_element_type=f32).astype(bf16)
        return carry

    lax.fori_loop(0, width // TILE, finish, 0)

    def all_sent(ref, sem):
        pltpu.make_async_copy(ref, ref, sem).wait()

    all_sent(full.at[pl.ds(0, GROUP - 1), :, cols_a], sent_a)
    all_sent(full.at[pl.ds(0, GROUP - 1), :, cols_b], sent_b)
    all_sent(send_one.at[pl.ds(0, NZ - 1)], one_sent)
    all_sent(send_two.at[pl.ds(0, NY * NC - 1)], two_sent)
    for step in range(1, NX):
        copy_small(small_out, small_in, small_sent, small_recv, step).wait_send()
        copy_small(inner_out, inner_in, inner_sent, inner_recv, step).wait_send()
        for part in range(tiles_x):
            copy_part(step, part).wait_send()
            copy_resid(step, part).wait_send()


def on_device(token_shard, token_row, table, gain, key_value_weight, kv_target):
    tokens = token_row.shape[0]
    depth, width = key_value_weight.shape
    kept = kv_target.shape[1]
    slots = 2 * tokens
    parts = kept // TILE
    bf16, f32 = jnp.bfloat16, jnp.float32
    dma = pltpu.SemaphoreType.DMA
    vmem = pl.BlockSpec(memory_space=pltpu.VMEM)
    anywhere = pl.BlockSpec(memory_space=pl.ANY)
    return pl.pallas_call(
        kernel,
        out_shape=jax.ShapeDtypeStruct(table.shape, bf16),
        in_specs=[vmem] * 5 + [anywhere] * 2,
        out_specs=vmem,
        scratch_shapes=[
            pltpu.VMEM((GROUP, depth, width), bf16),
            pltpu.VMEM(table.shape, bf16),
            pltpu.VMEM((NZ, slots // NZ, kept + IDS), bf16),
            pltpu.VMEM((NZ, slots // NZ, kept + IDS), bf16),
            pltpu.VMEM((NY * NC, slots // (NY * NC), kept + IDS), bf16),
            pltpu.VMEM((NY * NC, slots // (NY * NC), kept + IDS), bf16),
            pltpu.VMEM((slots, width), bf16),
            pltpu.VMEM((slots, width), bf16),
            pltpu.VMEM((parts, slots, TILE), f32),
            pltpu.VMEM((NX - 1, parts, slots, TILE), bf16),
            pltpu.VMEM((NX - 1, parts, slots, TILE), bf16),
            pltpu.VMEM((NX, parts, slots, TILE), bf16),
            pltpu.VMEM((8, slots), f32),
            pltpu.VMEM((NX - 1, 8, slots), f32),
            pltpu.VMEM((8, slots), f32),
            pltpu.VMEM((NX - 1, 8, slots), f32),
            dma,
            dma,
            dma((GROUP,)),
            dma((GROUP,)),
            dma,
            dma,
            dma((NZ,)),
            dma,
            dma((NY * NC,)),
            dma,
            dma((NX - 1,)),
            dma((NX - 1,)),
            dma((NX - 1, parts)),
            dma((NX - 1, parts)),
            dma((NX - 1, parts)),
            dma((NX - 1, parts)),
            dma((NX - 1,)),
            dma((NX - 1,)),
        ],
        compiler_params=pltpu.CompilerParams(
            collective_id=0, has_side_effects=True, vmem_limit_bytes=48 * 2**20
        ),
    )(
        token_shard,
        token_shard.reshape(1, tokens),
        token_row.reshape(tokens, 1),
        kv_target,
        gain.reshape(1, width),
        key_value_weight,
        table,
    )


def solution(mesh):
    return jax.shard_map(
        on_device,
        mesh=mesh,
        in_specs=(
            P(("section", "wide"), None),
            P(("section", "wide")),
            P(("section", "wide"), "narrow"),
            P("narrow"),
            P(("section", "wide"), "narrow"),
            P(("section", "wide"), "narrow"),
        ),
        out_specs=P(("section", "wide"), "narrow"),
        check_vma=False,
    )
```

```python
import functools

import jax
import jax.numpy as jnp
from jax import lax
from jax.experimental import pallas as pl
from jax.experimental.pallas import tpu as pltpu
from jax.sharding import PartitionSpec as P

MESH = pl.DeviceIdType.MESH
D = 8192
EPSILON = 1e-05
NY, NZ, NC, NX = 4, 16, 2, 4
GROUP = NY * NZ * NC
SPLIT = 512
TILE = 256
PART = 128
HALF = 128
TURNS = 8


def kernel(
    shard_hbm,
    row_hbm,
    target_hbm,
    gain_hbm,
    weight_hbm,
    table_hbm,
    out_ref,
    shard,
    row,
    target,
    gain,
    full,
    table,
    ids_out,
    ids_mid,
    ids_all,
    ids_in,
    goal_out,
    goal_mid,
    goal_next,
    goal,
    hidden,
    normed,
    partial,
    half_out,
    half_in,
    joint_out,
    joint_in,
    resid,
    inner,
    back,
    square_out,
    square_in,
    inner_out,
    inner_in,
    local_sem,
    recv_a,
    recv_b,
    sent_a,
    sent_b,
    idy_recv,
    idz_recv,
    goaly_recv,
    goalz_recv,
    many_sent,
    square_recv,
    square_sent,
    inner_recv,
    inner_sent,
    half_recv,
    half_sent,
    joint_recv,
    joint_sent,
    resid_recv,
    resid_sent,
):
    f32, bf16, i32 = jnp.float32, jnp.bfloat16, jnp.int32
    section, wide, x = lax.axis_index("section"), lax.axis_index("wide"), lax.axis_index("narrow")
    z, c = wide // 4, wide % 2
    y = section * 2 + (wide // 2) % 2
    here = y * 2 + c
    tokens, kept = target.shape
    slots = normed.shape[0]
    depth, width = full.shape[1:]
    rows_here = table.shape[0]
    cols_a, cols_b = pl.ds(0, SPLIT), pl.ds(SPLIT, width - SPLIT)
    spots = NY * NC
    per_y, per_z = slots // spots, slots // NZ

    def device(yy, zz, cc, xx):
        return (yy // 2, zz * 4 + (yy % 2) * 2 + cc, xx)

    def block(yy, zz, cc):
        return (yy // 2) * (NZ * 4) + zz * 4 + (yy % 2) * 2 + cc

    def yy_of(step):
        return lax.rem(y + step + NY, NY)

    def zz_of(step):
        return lax.rem(z + step + NZ, NZ)

    def xx_of(step):
        return lax.rem(x + step + NX, NX)

    def beside(xx):
        return device(y, z, c, xx)

    def remote(source, landing, sent, recv, to):
        return pltpu.make_async_remote_copy(
            src_ref=source, dst_ref=landing, send_sem=sent, recv_sem=recv, device_id=to, device_id_type=MESH
        )

    loads = [
        pltpu.make_async_copy(source, landing, local_sem.at[number])
        for number, (source, landing) in enumerate(
            (
                (shard_hbm, shard),
                (row_hbm, row),
                (weight_hbm, full.at[block(y, z, c)]),
                (target_hbm, target),
                (gain_hbm, gain),
                (table_hbm, table),
            )
        )
    ]
    for load in loads:
        load.start()

    barrier = pltpu.get_barrier_semaphore()

    def greet_z(step, carry):
        pl.semaphore_signal(barrier, inc=1, device_id=device(y, zz_of(step), c, x), device_id_type=MESH)
        return carry

    lax.fori_loop(1, NZ, greet_z, 0)

    def greet_y(step, carry):
        other = lax.rem(here + step, spots)
        pl.semaphore_signal(barrier, inc=1, device_id=device(other // 2, z, other % 2, x), device_id_type=MESH)
        return carry

    lax.fori_loop(1, spots, greet_y, 0)
    for step in range(1, NX):
        pl.semaphore_signal(barrier, inc=1, device_id=beside(xx_of(step)), device_id_type=MESH)

    loads[0].wait()
    loads[1].wait()
    first = lax.broadcasted_iota(i32, (tokens, tokens), 0)
    second = lax.broadcasted_iota(i32, (tokens, tokens), 1)
    holder = shard[...]
    holder_col = jnp.sum(jnp.where(first == second, holder, 0), axis=1, keepdims=True)
    same = jnp.logical_and(holder_col == holder, first < second)
    rank = jnp.sum(jnp.where(same, 1, 0), axis=0, keepdims=True)
    hold_z = (holder // 4) % NZ
    hold_y = (holder // 64) * 4 + holder % 4
    slot_of = hold_y * per_y + hold_z * 2 + rank
    placed = lax.broadcasted_iota(i32, (slots, tokens), 0) == slot_of
    slot_id = jnp.sum(jnp.where(placed, row[...] + 1, 0), axis=1, keepdims=True).astype(f32)
    spread_ids = lax.broadcasted_iota(i32, (per_y, 128), 0) == lax.broadcasted_iota(i32, (per_y, 128), 1)
    for spot in range(spots):
        line = jnp.sum(
            jnp.where(spread_ids, slot_id[spot * per_y : (spot + 1) * per_y], 0.0), axis=0, keepdims=True
        )
        ids_out[spot] = jnp.broadcast_to(line, (8, 128))
    loads[3].wait()
    place = jnp.where(placed, 1.0, 0.0).astype(bf16)
    goal_out[...] = (
        jnp.dot(place, target[...], preferred_element_type=f32).astype(bf16).reshape(spots, per_y, kept)
    )
    loads[2].wait()

    pl.semaphore_wait(barrier, (NZ - 1) + (spots - 1) + (NX - 1))

    def spot_device(spot):
        return device(spot // 2, z, spot % 2, x)

    def copy_idy(to, source):
        return remote(ids_out.at[to], ids_mid.at[source], many_sent.at[0], idy_recv.at[source], spot_device(to))

    def copy_idz(to, source):
        return remote(ids_all, ids_in.at[source], many_sent.at[1], idz_recv.at[source], device(y, to, c, x))

    def copy_goaly(to, source):
        return remote(goal_out.at[to], goal_mid.at[source], many_sent.at[2], goaly_recv.at[source], spot_device(to))

    def copy_goalz(to, source):
        return remote(goal_next.at[to], goal.at[source], many_sent.at[3], goalz_recv.at[source], device(y, to, c, x))

    def copy_weight(which, yy, zz, cc, to):
        cols, recv, sent = (cols_a, recv_a, sent_a) if which == "a" else (cols_b, recv_b, sent_b)
        piece = full.at[block(yy, zz, cc), :, cols]
        return remote(piece, piece, sent, recv.at[block(yy, zz, cc)], to)

    above, below = device(yy_of(1), z, c, x), device(yy_of(-1), z, c, x)
    opposite = device(yy_of(2), z, c, x)
    after, before = device(y, zz_of(1), c, x), device(y, zz_of(-1), c, x)
    partner = device(y, z, 1 - c, x)

    def pass_on(which, yy, zz, targets):
        for to in targets:
            copy_weight(which, yy, zz, c, to).start()

    def arrive(which, yy, zz, cc):
        copy_weight(which, yy, zz, cc, partner).wait_recv()

    def each(low, high, act):
        def step(index, carry):
            act(index)
            return carry

        lax.fori_loop(low, high, step, 0)

    def around(step):
        return lax.rem(here + step, spots)

    pass_on("b", y, z, (after, before))
    pass_on("a", y, z, (above, below, opposite))
    each(1, spots, lambda step: copy_idy(around(step), here).start())
    each(1, spots, lambda step: copy_goaly(around(step), here).start())
    pass_on("b", y, z, (above, below))
    pass_on("a", y, z, (after, before, partner))
    pass_on("b", y, z, (partner,))
    ids_mid[here] = ids_out[here]
    goal_mid[here] = goal_out[here]

    def when(condition, act):
        if isinstance(condition, bool):
            if condition:
                act()
        else:
            pl.when(condition)(act)

    def onward(which, yy, zz, sign, ahead):
        to = after if sign < 0 else before
        when(ahead, lambda: pass_on(which, yy, zz, (to,)))

    def first_hand(distance, sign, ahead):
        zz = zz_of(sign * distance)
        arrive("b", y, zz, c)
        onward("b", y, zz, sign, ahead)
        pass_on("b", y, zz, (above, below, partner))

    def planes(distance, sign, ahead):
        zz = zz_of(sign * distance)
        for step in range(NY):
            arrive("a", yy_of(step), zz, c)
            onward("a", yy_of(step), zz, sign, ahead)
            pass_on("a", yy_of(step), zz, (partner,))

    def second_hand(distance, sign):
        zz = zz_of(sign * distance)
        arrive("b", yy_of(-1), zz, c)
        when(distance % 2 == 0, lambda: pass_on("b", yy_of(-1), zz, (above,)))
        pass_on("b", yy_of(-1), zz, (partner,))
        arrive("b", yy_of(1), zz, c)
        when(distance % 2 == 1, lambda: pass_on("b", yy_of(1), zz, (below,)))
        pass_on("b", yy_of(1), zz, (partner,))

    def third_hand(distance, sign):
        zz = zz_of(sign * distance)
        arrive("b", yy_of(2), zz, c)
        pass_on("b", yy_of(2), zz, (partner,))

    def later(hand, distance):
        if isinstance(distance, int):
            if distance >= 0:
                hand(distance, -1)
            if 1 <= distance < NZ // 2:
                hand(distance, 1)
            return
        pl.when(distance >= 0)(lambda: hand(distance, -1))
        pl.when(distance >= 1)(lambda: hand(distance, 1))

    def send_goal(step):
        copy_goalz(zz_of(step), z).start()

    def spread(distance):
        first_hand(distance, -1, True)
        first_hand(distance, 1, distance < NZ // 2 - 1)

        @pl.when(distance <= 4)
        def _():
            for step in (11, 10):
                send_goal(step - 2 * distance)
                send_goal(2 * distance - step)

        planes(distance - 1, -1, True)
        planes(distance - 1, 1, True)
        later(second_hand, distance - 1)
        later(third_hand, distance - 2)

    first_hand(1, -1, True)
    first_hand(1, 1, True)
    each(1, spots, lambda step: copy_idy(here, around(step)).wait_recv())
    ids_all[...] = jnp.concatenate([ids_mid[spot][0:1, :] for spot in range(spots)], axis=0)
    each(1, NZ, lambda step: copy_idz(zz_of(step), z).start())
    ids_in[z] = ids_all[...]
    for step in range(1, NY):
        arrive("a", yy_of(step), z, c)
        pass_on("a", yy_of(step), z, (after, before, partner))

    each(1, spots, lambda step: copy_goaly(here, around(step)).wait_recv())
    out_slot = lax.broadcasted_iota(i32, (slots, slots), 0)
    in_slot = lax.broadcasted_iota(i32, (slots, slots), 1)
    inside = out_slot % per_z
    from_slot = (inside % spots) * per_y + (out_slot // per_z) * 2 + inside // spots
    order = jnp.where(in_slot == from_slot, 1.0, 0.0).astype(bf16)
    arrived = goal_mid[...].reshape(slots, kept)
    goal_next[...] = jnp.dot(order, arrived, preferred_element_type=f32).astype(bf16).reshape(NZ, per_z, kept)
    send_goal(NZ // 2)
    goal[z] = goal_next[z]

    second_hand(0, -1)
    each(2, 3, spread)

    each(1, NZ, lambda step: copy_idz(z, zz_of(step)).wait_recv())
    loads[5].wait()
    loads[4].wait()
    listed = ids_in[...].reshape(NZ * spots, 128)
    lane = lax.broadcasted_iota(i32, listed.shape, 1)
    wanted = (
        jnp.concatenate(
            [
                jnp.sum(jnp.where(lane == 2 * z + k, listed, 0.0), axis=1, keepdims=True).reshape(NZ, spots, 1)
                for k in range(2)
            ],
            axis=1,
        ).reshape(slots, 1)
        - 1.0
    )
    pick = jnp.where(lax.broadcasted_iota(i32, (slots, rows_here), 1).astype(f32) == wanted, 1.0, 0.0).astype(bf16)
    square_sum = jnp.zeros((slots, 1), f32)
    for tile in range(width // 512):
        at = pl.ds(tile * 512, 512)
        picked = jnp.dot(pick, table[:, at], preferred_element_type=f32)
        hidden[:, at] = picked.astype(bf16)
        square_sum += jnp.sum(picked * picked, axis=1, keepdims=True)
    diagonal = out_slot == in_slot

    def as_row(column):
        return jnp.sum(jnp.where(diagonal, column, 0.0), axis=0, keepdims=True)

    def as_column(line):
        return jnp.sum(jnp.where(diagonal, line, 0.0), axis=1, keepdims=True)

    def copy_square(step):
        return remote(
            square_out, square_in.at[step - 1], square_sent.at[step - 1], square_recv.at[step - 1], beside(xx_of(step))
        )

    def copy_inner(step):
        return remote(
            inner_out, inner_in.at[step - 1], inner_sent.at[step - 1], inner_recv.at[step - 1], beside(xx_of(step))
        )

    square_row = as_row(square_sum)
    square_out[...] = jnp.broadcast_to(square_row, square_out.shape)
    for step in range(1, NX):
        copy_square(step).start()

    each(3, 4, spread)

    for step in range(1, NX):
        copy_square(step).wait_recv()
    total = square_row
    for step in range(1, NX):
        total += square_in[step - 1][0:1, :]
    row_scale = lax.rsqrt(as_column(total) / D + EPSILON)
    for tile in range(width // 512):
        at = pl.ds(tile * 512, 512)
        normed[:, at] = (hidden[:, at].astype(f32) * row_scale * gain[:, at]).astype(bf16)

    pairs = NZ // 2
    mine, lean = z // 2, 1 - 2 * (z % 2)
    pair_at = [
        lax.rem(mine + lean * (-((turn + 1) // 2) if turn % 2 else turn // 2) + pairs, pairs) for turn in range(TURNS)
    ]
    blocks = PART // depth
    right, left = xx_of(1), xx_of(-1)

    def tile_rows(part, pair):
        return pl.ds((part * pairs + pair) * blocks, blocks)

    def ends_here(pair):
        return x % 2 == pair // (pairs // 2)

    def copy_half(turn, side):
        return remote(
            half_out.at[turn, side],
            half_in.at[turn, side],
            half_sent.at[turn, side],
            half_recv.at[turn, side],
            beside(left if side else right),
        )

    def copy_joint(turn, side):
        return remote(
            joint_out.at[turn, side],
            joint_in.at[turn, side],
            joint_sent.at[turn, side],
            joint_recv.at[turn, side],
            beside(left if side else right),
        )

    def part_cols(part):
        return pl.ds(pl.multiple_of(part * PART, PART), PART)

    def side_rows(side):
        return pl.ds(side * HALF, HALF)

    def copy_resid(turn, part, side):
        piece = resid.at[turn, :, part_cols(part)]
        return remote(
            piece, piece, resid_sent.at[turn, side], resid_recv.at[turn, part, 0], beside(left if side else right)
        )

    def copy_resid_half(turn, part, side):
        piece = resid.at[turn, side_rows(side), part_cols(part)]
        return remote(
            piece, piece, resid_sent.at[turn, side], resid_recv.at[turn, part, side], beside(left if side else right)
        )

    def project(turn):
        pair = pair_at[turn]
        for step in range(2):
            for yy in range(NY):
                arrive("a", yy, pair * 2 + step, 1 - c)
                arrive("b", yy, pair * 2 + step, 1 - c)
        dest = ends_here(pair)
        order = (jnp.where(dest, 1 - x // 2, right // 2), jnp.where(dest, x // 2, left // 2))
        rows = jnp.concatenate([full[tile_rows(part, pair)].reshape(PART, width) for part in order], axis=0)
        partial[turn] = lax.dot_general(normed[...], rows, (((1,), (1,)), ((), ())), preferred_element_type=f32)

        @pl.when(dest)
        def _():
            for side in range(2):
                half_out[turn, side] = partial[turn, side_rows(side), 0:PART].astype(bf16)
                copy_half(turn, side).start()

    def relay_sums(turn):
        @pl.when(jnp.logical_not(ends_here(pair_at[turn])))
        def _():
            for side in range(2):
                copy_half(turn, side).wait_recv()
                near, far, at = side_rows(side), side_rows(1 - side), slice(side * PART, (side + 1) * PART)
                joint_out[turn, side, near] = (partial[turn, near, at] + half_in[turn, side].astype(f32)).astype(bf16)
                joint_out[turn, side, far] = partial[turn, far, at].astype(bf16)
                copy_joint(turn, side).start()

    def subtract(turn):
        pair = pair_at[turn]

        @pl.when(ends_here(pair))
        def _():
            for side in range(2):
                copy_joint(turn, side).wait_recv()
            projected = partial[turn, :, PART:] + joint_in[turn, 0].astype(f32) + joint_in[turn, 1].astype(f32)
            wished = goal[:, :, part_cols(pair % (pairs // 2))].reshape(slots, PART)
            residual = (projected - wished.astype(f32)).astype(bf16)
            resid[turn, :, part_cols(x // 2)] = residual
            for side in range(2):
                copy_resid(turn, x // 2, side).start()
            inner[...] += projected * residual.astype(f32)

    def relay_resid(turn):
        @pl.when(jnp.logical_not(ends_here(pair_at[turn])))
        def _():
            copy_resid(turn, left // 2, 0).wait_recv()
            copy_resid_half(turn, left // 2, 0).start()
            copy_resid(turn, right // 2, 1).wait_recv()
            copy_resid_half(turn, right // 2, 1).start()

    def await_resid(turn):
        @pl.when(ends_here(pair_at[turn]))
        def _():
            for side in range(2):
                copy_resid_half(turn, 1 - x // 2, side).wait_recv()

    def step_back(turn, at):
        rows = jnp.concatenate(
            [full[tile_rows(part, pair_at[turn]), :, at].reshape(PART, at.size) for part in range(2)], axis=0
        )
        return jnp.dot(resid[turn], rows, preferred_element_type=f32)

    def accumulate(turns):
        for turn in turns:
            await_resid(turn)

        def add(tile):
            at = pl.ds(pl.multiple_of(tile * TILE, TILE), TILE)
            total = step_back(turns[0], at) if turns[0] == 0 else back[:, at] + step_back(turns[0], at)
            for turn in turns[1:]:
                total += step_back(turn, at)
            back[:, at] = total

        each(0, width // TILE, add)

    inner[...] = jnp.zeros(inner.shape, f32)
    far = NZ // 2
    jobs = {
        4: ((project, 0), None, None, None),
        5: ((project, 1), (relay_sums, 0), None, None),
        6: ((project, 2), (relay_sums, 1), None, (subtract, 0)),
        7: ((project, 3), (relay_sums, 2), (subtract, 1), (relay_resid, 0)),
        8: ((project, 4), (relay_sums, 3), (subtract, 2), (relay_resid, 1)),
        9: ((project, 5), (relay_sums, 4), (subtract, 3), (relay_resid, 2)),
        10: ((project, 6), (relay_sums, 5), (subtract, 4), (relay_resid, 3)),
    }

    def work(job):
        if job is not None:
            job[0](job[1])

    for distance in range(4, far + 3):
        if distance <= far:
            first_hand(distance, -1, distance < far)
            if distance < far:
                first_hand(distance, 1, distance < far - 1)
        if distance == 4:
            for step in (3, -3, 2, -2):
                send_goal(step)
        if distance == 5:
            for step in (1, -1):
                send_goal(step)
        work(jobs[distance][0])
        if distance - 1 <= far:
            planes(distance - 1, -1, distance - 1 < far)
            if distance - 1 < far:
                planes(distance - 1, 1, distance - 1 < far - 1)
        work(jobs[distance][1])
        if distance - 1 <= far:
            later(second_hand, distance - 1)
        work(jobs[distance][2])
        later(third_hand, distance - 2)
        if distance == 6:
            each(1, NZ, lambda step: copy_goalz(z, zz_of(step)).wait_recv())
        work(jobs[distance][3])
    project(7)
    relay_sums(6)
    subtract(5)
    relay_resid(4)
    accumulate((0, 1))
    relay_sums(7)
    subtract(6)
    relay_resid(5)
    subtract(7)

    inner_row = as_row(jnp.sum(inner[...], axis=1, keepdims=True))
    inner_out[...] = jnp.broadcast_to(inner_row, inner_out.shape)
    for step in range(1, NX):
        copy_inner(step).start()
    relay_resid(6)
    accumulate((2, 3, 4, 5))
    relay_resid(7)
    wanted_row = as_row(wanted)
    put = jnp.where(lax.broadcasted_iota(i32, (rows_here, slots), 0).astype(f32) == wanted_row, 1.0, 0.0).astype(bf16)
    for step in range(1, NX):
        copy_inner(step).wait_recv()
    inner_all = inner_row
    for step in range(1, NX):
        inner_all += inner_in[step - 1][0:1, :]
    pull = row_scale * row_scale * as_column(inner_all) / D
    await_resid(6)
    await_resid(7)

    def finish(tile):
        at = pl.ds(pl.multiple_of(tile * TILE, TILE), TILE)
        weighted = (back[:, at] + step_back(6, at) + step_back(7, at)) * gain[:, at]
        grad = (row_scale * weighted - hidden[:, at].astype(f32) * pull).astype(bf16)
        out_ref[:, at] = jnp.dot(put, grad, preferred_element_type=f32).astype(bf16)

    each(0, width // TILE, finish)

    def all_sent(ref, sem):
        pltpu.make_async_copy(ref, ref, sem).wait()

    all_sent(full.at[pl.ds(0, GROUP - 1), :, cols_a], sent_a)
    all_sent(full.at[pl.ds(0, GROUP - 1), :, cols_b], sent_b)
    all_sent(ids_out.at[pl.ds(0, spots - 1)], many_sent.at[0])
    all_sent(ids_in.at[pl.ds(0, NZ - 1)], many_sent.at[1])
    all_sent(goal_out.at[pl.ds(0, spots - 1)], many_sent.at[2])
    all_sent(goal_next.at[pl.ds(0, NZ - 1)], many_sent.at[3])
    for step in range(1, NX):
        copy_square(step).wait_send()
        copy_inner(step).wait_send()
    for turn in range(TURNS):
        dest = ends_here(pair_at[turn])

        @pl.when(dest)
        def _():
            for side in range(2):
                copy_half(turn, side).wait_send()
                copy_resid(turn, x // 2, side).wait_send()

        @pl.when(jnp.logical_not(dest))
        def _():
            copy_resid_half(turn, left // 2, 0).wait_send()
            copy_resid_half(turn, right // 2, 1).wait_send()
            for side in range(2):
                copy_joint(turn, side).wait_send()


def on_device(token_shard, token_row, table, gain, key_value_weight, kv_target):
    tokens = token_row.shape[0]
    depth, width = key_value_weight.shape
    kept = kv_target.shape[1]
    slots = 2 * tokens
    spots = NY * NC
    bf16, f32, i32 = jnp.bfloat16, jnp.float32, jnp.int32
    dma, vmem = pltpu.SemaphoreType.DMA, pltpu.VMEM
    outside = pl.BlockSpec(memory_space=pltpu.HBM)
    return pl.pallas_call(
        kernel,
        out_shape=jax.ShapeDtypeStruct(table.shape, bf16),
        in_specs=[outside] * 6,
        out_specs=pl.BlockSpec(memory_space=vmem),
        scratch_shapes=[
            vmem((1, tokens), i32),
            vmem((1, tokens), i32),
            vmem((tokens, kept), bf16),
            vmem((1, width), f32),
            vmem((GROUP, depth, width), bf16),
            vmem(table.shape, bf16),
            vmem((spots, 8, 128), f32),
            vmem((spots, 8, 128), f32),
            vmem((spots, 128), f32),
            vmem((NZ, spots, 128), f32),
            vmem((spots, slots // spots, kept), bf16),
            vmem((spots, slots // spots, kept), bf16),
            vmem((NZ, slots // NZ, kept), bf16),
            vmem((NZ, slots // NZ, kept), bf16),
            vmem((slots, width), bf16),
            vmem((slots, width), bf16),
            vmem((TURNS, slots, 2 * PART), f32),
            vmem((TURNS, 2, HALF, PART), bf16),
            vmem((TURNS, 2, HALF, PART), bf16),
            vmem((TURNS, 2, slots, PART), bf16),
            vmem((TURNS, 2, slots, PART), bf16),
            vmem((TURNS, slots, 2 * PART), bf16),
            vmem((slots, PART), f32),
            vmem((slots, width), f32),
            vmem((8, slots), f32),
            vmem((NX - 1, 8, slots), f32),
            vmem((8, slots), f32),
            vmem((NX - 1, 8, slots), f32),
            dma((6,)),
            dma((GROUP,)),
            dma((GROUP,)),
            dma,
            dma,
            dma((spots,)),
            dma((NZ,)),
            dma((spots,)),
            dma((NZ,)),
            dma((4,)),
            dma((NX - 1,)),
            dma((NX - 1,)),
            dma((NX - 1,)),
            dma((NX - 1,)),
            dma((TURNS, 2)),
            dma((TURNS, 2)),
            dma((TURNS, 2)),
            dma((TURNS, 2)),
            dma((TURNS, 2, 2)),
            dma((TURNS, 2)),
        ],
        compiler_params=pltpu.CompilerParams(
            collective_id=0, has_side_effects=True, vmem_limit_bytes=59936 * 1024
        ),
    )(
        token_shard.reshape(1, tokens),
        token_row.reshape(1, tokens),
        kv_target,
        gain.reshape(1, width),
        key_value_weight,
        table,
    )


def solution(mesh):
    return jax.shard_map(
        on_device,
        mesh=mesh,
        in_specs=(
            P(("section", "wide"), None),
            P(("section", "wide")),
            P(("section", "wide"), "narrow"),
            P("narrow"),
            P(("section", "wide"), "narrow"),
            P(("section", "wide"), "narrow"),
        ),
        out_specs=P(("section", "wide"), "narrow"),
        check_vma=False,
    )
```

```python
import functools

import jax
import jax.numpy as jnp
from jax import lax
from jax.experimental import pallas as pl
from jax.experimental.pallas import tpu as pltpu
from jax.sharding import PartitionSpec as P

MESH = pl.DeviceIdType.MESH
D = 8192
EPSILON = 1e-05
NY, NZ, NC, NX = 4, 16, 2, 4
GROUP = NY * NZ * NC
SPLIT = 512
TILE = 256
PART = 128
DIRECT = (6, 7)
HALF = 128
TURNS = 8


def kernel(
    shard_hbm,
    row_hbm,
    target_hbm,
    gain_hbm,
    weight_hbm,
    table_hbm,
    grad_ref,
    wanted_ref,
    shard,
    row,
    target,
    gain,
    full,
    table,
    ids_out,
    ids_mid,
    ids_all,
    ids_in,
    goal_out,
    goal_mid,
    goal_next,
    goal,
    hidden,
    normed,
    partial,
    half_out,
    half_in,
    joint_out,
    joint_in,
    direct_out,
    direct_in,
    resid,
    inner,
    back,
    square_out,
    square_in,
    inner_out,
    inner_in,
    local_sem,
    recv_a,
    recv_b,
    sent_a,
    sent_b,
    idy_recv,
    idz_recv,
    goaly_recv,
    goalz_recv,
    many_sent,
    square_recv,
    square_sent,
    inner_recv,
    inner_sent,
    half_recv,
    half_sent,
    joint_recv,
    joint_sent,
    resid_recv,
    resid_sent,
    direct_recv,
    direct_sent,
    across_sent,
):
    f32, bf16, i32 = jnp.float32, jnp.bfloat16, jnp.int32
    section, wide, x = lax.axis_index("section"), lax.axis_index("wide"), lax.axis_index("narrow")
    z, c = wide // 4, wide % 2
    y = section * 2 + (wide // 2) % 2
    here = y * 2 + c
    tokens, kept = target.shape
    slots = normed.shape[0]
    depth, width = full.shape[1:]
    rows_here = table.shape[0]
    cols_a, cols_b = pl.ds(0, SPLIT), pl.ds(SPLIT, width - SPLIT)
    spots = NY * NC
    per_y, per_z = slots // spots, slots // NZ

    def device(yy, zz, cc, xx):
        return (yy // 2, zz * 4 + (yy % 2) * 2 + cc, xx)

    def block(yy, zz, cc):
        return (yy // 2) * (NZ * 4) + zz * 4 + (yy % 2) * 2 + cc

    def yy_of(step):
        return lax.rem(y + step + NY, NY)

    def zz_of(step):
        return lax.rem(z + step + NZ, NZ)

    def xx_of(step):
        return lax.rem(x + step + NX, NX)

    def beside(xx):
        return device(y, z, c, xx)

    def remote(source, landing, sent, recv, to):
        return pltpu.make_async_remote_copy(
            src_ref=source, dst_ref=landing, send_sem=sent, recv_sem=recv, device_id=to, device_id_type=MESH
        )

    loads = [
        pltpu.make_async_copy(source, landing, local_sem.at[number])
        for number, (source, landing) in enumerate(
            (
                (shard_hbm, shard),
                (row_hbm, row),
                (weight_hbm, full.at[block(y, z, c)]),
                (target_hbm, target),
                (gain_hbm, gain),
                (table_hbm, table),
            )
        )
    ]
    for load in loads:
        load.start()

    barrier = pltpu.get_barrier_semaphore()

    def greet_z(step, carry):
        pl.semaphore_signal(barrier, inc=1, device_id=device(y, zz_of(step), c, x), device_id_type=MESH)
        return carry

    lax.fori_loop(1, NZ, greet_z, 0)

    def greet_y(step, carry):
        other = lax.rem(here + step, spots)
        pl.semaphore_signal(barrier, inc=1, device_id=device(other // 2, z, other % 2, x), device_id_type=MESH)
        return carry

    lax.fori_loop(1, spots, greet_y, 0)
    for step in range(1, NX):
        pl.semaphore_signal(barrier, inc=1, device_id=beside(xx_of(step)), device_id_type=MESH)

    loads[0].wait()
    loads[1].wait()
    first = lax.broadcasted_iota(i32, (tokens, tokens), 0)
    second = lax.broadcasted_iota(i32, (tokens, tokens), 1)
    holder = shard[...]
    holder_col = jnp.sum(jnp.where(first == second, holder, 0), axis=1, keepdims=True)
    same = jnp.logical_and(holder_col == holder, first < second)
    rank = jnp.sum(jnp.where(same, 1, 0), axis=0, keepdims=True)
    hold_z = (holder // 4) % NZ
    hold_y = (holder // 64) * 4 + holder % 4
    slot_of = hold_y * per_y + hold_z * 2 + rank
    placed = lax.broadcasted_iota(i32, (slots, tokens), 0) == slot_of
    slot_id = jnp.sum(jnp.where(placed, row[...] + 1, 0), axis=1, keepdims=True).astype(f32)
    spread_ids = lax.broadcasted_iota(i32, (per_y, 128), 0) == lax.broadcasted_iota(i32, (per_y, 128), 1)
    for spot in range(spots):
        line = jnp.sum(
            jnp.where(spread_ids, slot_id[spot * per_y : (spot + 1) * per_y], 0.0), axis=0, keepdims=True
        )
        ids_out[spot] = jnp.broadcast_to(line, (8, 128))
    loads[3].wait()
    place = jnp.where(placed, 1.0, 0.0).astype(bf16)
    goal_out[...] = (
        jnp.dot(place, target[...], preferred_element_type=f32).astype(bf16).reshape(spots, per_y, kept)
    )
    loads[2].wait()

    pl.semaphore_wait(barrier, (NZ - 1) + (spots - 1) + (NX - 1))

    def spot_device(spot):
        return device(spot // 2, z, spot % 2, x)

    def copy_idy(to, source):
        return remote(ids_out.at[to], ids_mid.at[source], many_sent.at[0], idy_recv.at[source], spot_device(to))

    def copy_idz(to, source):
        return remote(ids_all, ids_in.at[source], many_sent.at[1], idz_recv.at[source], device(y, to, c, x))

    def copy_goaly(to, source):
        return remote(goal_out.at[to], goal_mid.at[source], many_sent.at[2], goaly_recv.at[source], spot_device(to))

    def copy_goalz(to, source):
        return remote(goal_next.at[to], goal.at[source], many_sent.at[3], goalz_recv.at[source], device(y, to, c, x))

    def copy_weight(which, yy, zz, cc, to):
        cols, recv, sent = (cols_a, recv_a, sent_a) if which == "a" else (cols_b, recv_b, sent_b)
        piece = full.at[block(yy, zz, cc), :, cols]
        return remote(piece, piece, sent, recv.at[block(yy, zz, cc)], to)

    above, below = device(yy_of(1), z, c, x), device(yy_of(-1), z, c, x)
    opposite = device(yy_of(2), z, c, x)
    after, before = device(y, zz_of(1), c, x), device(y, zz_of(-1), c, x)
    partner = device(y, z, 1 - c, x)

    def pass_on(which, yy, zz, targets):
        for to in targets:
            copy_weight(which, yy, zz, c, to).start()

    def arrive(which, yy, zz, cc):
        copy_weight(which, yy, zz, cc, partner).wait_recv()

    def each(low, high, act):
        def step(index, carry):
            act(index)
            return carry

        lax.fori_loop(low, high, step, 0)

    def around(step):
        return lax.rem(here + step, spots)

    pass_on("b", y, z, (after, before))
    pass_on("a", y, z, (above, below, opposite))
    each(1, spots, lambda step: copy_idy(around(step), here).start())
    each(1, spots, lambda step: copy_goaly(around(step), here).start())
    pass_on("b", y, z, (above, below))
    pass_on("a", y, z, (after, before, partner))
    pass_on("b", y, z, (partner,))
    ids_mid[here] = ids_out[here]
    goal_mid[here] = goal_out[here]

    def when(condition, act):
        if isinstance(condition, bool):
            if condition:
                act()
        else:
            pl.when(condition)(act)

    def onward(which, yy, zz, sign, ahead):
        to = after if sign < 0 else before
        when(ahead, lambda: pass_on(which, yy, zz, (to,)))

    def first_hand(distance, sign, ahead):
        zz = zz_of(sign * distance)
        arrive("b", y, zz, c)
        onward("b", y, zz, sign, ahead)
        pass_on("b", y, zz, (above, below, partner))

    def planes(distance, sign, ahead):
        zz = zz_of(sign * distance)
        for step in range(NY):
            arrive("a", yy_of(step), zz, c)
            onward("a", yy_of(step), zz, sign, ahead)
            pass_on("a", yy_of(step), zz, (partner,))

    def second_hand(distance, sign):
        zz = zz_of(sign * distance)
        arrive("b", yy_of(-1), zz, c)
        when(distance % 2 == 0, lambda: pass_on("b", yy_of(-1), zz, (above,)))
        pass_on("b", yy_of(-1), zz, (partner,))
        arrive("b", yy_of(1), zz, c)
        when(distance % 2 == 1, lambda: pass_on("b", yy_of(1), zz, (below,)))
        pass_on("b", yy_of(1), zz, (partner,))

    def third_hand(distance, sign):
        zz = zz_of(sign * distance)
        arrive("b", yy_of(2), zz, c)
        pass_on("b", yy_of(2), zz, (partner,))

    def later(hand, distance):
        if isinstance(distance, int):
            if distance >= 0:
                hand(distance, -1)
            if 1 <= distance < NZ // 2:
                hand(distance, 1)
            return
        pl.when(distance >= 0)(lambda: hand(distance, -1))
        pl.when(distance >= 1)(lambda: hand(distance, 1))

    def send_goal(step):
        copy_goalz(zz_of(step), z).start()

    def both(hand, distance):
        hand(distance, -1, True)
        hand(distance, 1, True)

    both(first_hand, 1)
    for step in range(1, NY):
        arrive("a", yy_of(step), z, c)
        pass_on("a", yy_of(step), z, (after, before, partner))
    both(first_hand, 2)
    each(1, spots, lambda step: copy_idy(here, around(step)).wait_recv())
    ids_all[...] = jnp.concatenate([ids_mid[spot][0:1, :] for spot in range(spots)], axis=0)
    each(1, NZ, lambda step: copy_idz(zz_of(step), z).start())
    ids_in[z] = ids_all[...]
    both(planes, 1)
    later(second_hand, 0)

    each(1, spots, lambda step: copy_goaly(here, around(step)).wait_recv())
    out_slot = lax.broadcasted_iota(i32, (slots, slots), 0)
    in_slot = lax.broadcasted_iota(i32, (slots, slots), 1)
    inside = out_slot % per_z
    from_slot = (inside % spots) * per_y + (out_slot // per_z) * 2 + inside // spots
    order = jnp.where(in_slot == from_slot, 1.0, 0.0).astype(bf16)
    arrived = goal_mid[...].reshape(slots, kept)
    goal_next[...] = jnp.dot(order, arrived, preferred_element_type=f32).astype(bf16).reshape(NZ, per_z, kept)
    for step in (8, 7, -7, 6, -6):
        send_goal(step)
    goal[z] = goal_next[z]

    both(first_hand, 3)
    both(planes, 2)
    later(second_hand, 1)
    later(third_hand, 0)
    for step in (5, -5, 4, -4):
        send_goal(step)

    each(1, NZ, lambda step: copy_idz(z, zz_of(step)).wait_recv())
    loads[5].wait()
    loads[4].wait()
    listed = ids_in[...].reshape(NZ * spots, 128)
    lane = lax.broadcasted_iota(i32, listed.shape, 1)
    wanted = (
        jnp.concatenate(
            [
                jnp.sum(jnp.where(lane == 2 * z + k, listed, 0.0), axis=1, keepdims=True).reshape(NZ, spots, 1)
                for k in range(2)
            ],
            axis=1,
        ).reshape(slots, 1)
        - 1.0
    )
    pick = jnp.where(lax.broadcasted_iota(i32, (slots, rows_here), 1).astype(f32) == wanted, 1.0, 0.0).astype(bf16)
    square_sum = jnp.zeros((slots, 1), f32)
    for tile in range(width // 512):
        at = pl.ds(tile * 512, 512)
        picked = jnp.dot(pick, table[:, at], preferred_element_type=f32)
        hidden[:, at] = picked.astype(bf16)
        square_sum += jnp.sum(picked * picked, axis=1, keepdims=True)
    diagonal = out_slot == in_slot

    def as_row(column):
        return jnp.sum(jnp.where(diagonal, column, 0.0), axis=0, keepdims=True)

    def as_column(line):
        return jnp.sum(jnp.where(diagonal, line, 0.0), axis=1, keepdims=True)

    def copy_square(step):
        return remote(
            square_out, square_in.at[step - 1], square_sent.at[step - 1], square_recv.at[step - 1], beside(xx_of(step))
        )

    def copy_inner(step):
        return remote(
            inner_out, inner_in.at[step - 1], inner_sent.at[step - 1], inner_recv.at[step - 1], beside(xx_of(step))
        )

    square_row = as_row(square_sum)
    square_out[...] = jnp.broadcast_to(square_row, square_out.shape)
    for step in range(1, NX):
        copy_square(step).start()

    later(second_hand, 2)
    later(third_hand, 1)

    for step in range(1, NX):
        copy_square(step).wait_recv()
    total = square_row
    for step in range(1, NX):
        total += square_in[step - 1][0:1, :]
    row_scale = lax.rsqrt(as_column(total) / D + EPSILON)
    for tile in range(width // 512):
        at = pl.ds(tile * 512, 512)
        normed[:, at] = (hidden[:, at].astype(f32) * row_scale * gain[:, at]).astype(bf16)

    pairs = NZ // 2
    mine, lean = z // 2, 1 - 2 * (z % 2)
    pair_at = [
        lax.rem(mine + lean * (-((turn + 1) // 2) if turn % 2 else turn // 2) + pairs, pairs) for turn in range(TURNS)
    ]
    blocks = PART // depth
    right, left = xx_of(1), xx_of(-1)

    def copy_direct(turn):
        at = turn - DIRECT[0]
        return remote(direct_out.at[at], direct_in.at[at], direct_sent.at[at], direct_recv.at[at], beside(xx_of(2)))

    def copy_resid_across(turn, part):
        piece = resid.at[turn, :, part_cols(part)]
        return remote(
            piece, piece, across_sent.at[turn - DIRECT[0]], resid_recv.at[turn, part, 0], beside(xx_of(2))
        )

    def tile_rows(part, pair):
        return pl.ds((part * pairs + pair) * blocks, blocks)

    def ends_here(pair):
        return x % 2 == pair // (pairs // 2)

    def copy_half(turn, side):
        return remote(
            half_out.at[turn, side],
            half_in.at[turn, side],
            half_sent.at[turn, side],
            half_recv.at[turn, side],
            beside(left if side else right),
        )

    def copy_joint(turn, side):
        return remote(
            joint_out.at[turn, side],
            joint_in.at[turn, side],
            joint_sent.at[turn, side],
            joint_recv.at[turn, side],
            beside(left if side else right),
        )

    def part_cols(part):
        return pl.ds(pl.multiple_of(part * PART, PART), PART)

    def side_rows(side):
        return pl.ds(side * HALF, HALF)

    def copy_resid(turn, part, side):
        piece = resid.at[turn, :, part_cols(part)]
        return remote(
            piece, piece, resid_sent.at[turn, side], resid_recv.at[turn, part, 0], beside(left if side else right)
        )

    def copy_resid_half(turn, part, side):
        piece = resid.at[turn, side_rows(side), part_cols(part)]
        return remote(
            piece, piece, resid_sent.at[turn, side], resid_recv.at[turn, part, side], beside(left if side else right)
        )

    def project(turn):
        pair = pair_at[turn]
        for step in range(2):
            for yy in range(NY):
                arrive("a", yy, pair * 2 + step, 1 - c)
                arrive("b", yy, pair * 2 + step, 1 - c)
        dest = ends_here(pair)
        order = (jnp.where(dest, 1 - x // 2, right // 2), jnp.where(dest, x // 2, left // 2))
        rows = jnp.concatenate([full[tile_rows(part, pair)].reshape(PART, width) for part in order], axis=0)
        partial[turn] = lax.dot_general(normed[...], rows, (((1,), (1,)), ((), ())), preferred_element_type=f32)

        if turn in DIRECT:

            @pl.when(dest)
            def _():
                direct_out[turn - DIRECT[0]] = partial[turn, :, 0:PART].astype(bf16)
                copy_direct(turn).start()

            @pl.when(jnp.logical_not(dest))
            def _():
                for side in range(2):
                    joint_out[turn, side] = partial[turn, :, side * PART : (side + 1) * PART].astype(bf16)
                    copy_joint(turn, side).start()

            return

        @pl.when(dest)
        def _():
            for side in range(2):
                half_out[turn, side] = partial[turn, side_rows(side), 0:PART].astype(bf16)
                copy_half(turn, side).start()

    def relay_sums(turn):
        @pl.when(jnp.logical_not(ends_here(pair_at[turn])))
        def _():
            for side in range(2):
                copy_half(turn, side).wait_recv()
                near, far, at = side_rows(side), side_rows(1 - side), slice(side * PART, (side + 1) * PART)
                joint_out[turn, side, near] = (partial[turn, near, at] + half_in[turn, side].astype(f32)).astype(bf16)
                joint_out[turn, side, far] = partial[turn, far, at].astype(bf16)
                copy_joint(turn, side).start()

    def subtract(turn):
        pair = pair_at[turn]

        @pl.when(ends_here(pair))
        def _():
            for side in range(2):
                copy_joint(turn, side).wait_recv()
            projected = partial[turn, :, PART:] + joint_in[turn, 0].astype(f32) + joint_in[turn, 1].astype(f32)
            if turn in DIRECT:
                copy_direct(turn).wait_recv()
                projected += direct_in[turn - DIRECT[0]].astype(f32)
            wished = goal[:, :, part_cols(pair % (pairs // 2))].reshape(slots, PART)
            residual = (projected - wished.astype(f32)).astype(bf16)
            resid[turn, :, part_cols(x // 2)] = residual
            for side in range(2):
                copy_resid(turn, x // 2, side).start()
            if turn in DIRECT:
                copy_resid_across(turn, x // 2).start()
            inner[...] += projected * residual.astype(f32)

    def relay_resid(turn):
        @pl.when(jnp.logical_not(ends_here(pair_at[turn])))
        def _():
            copy_resid(turn, left // 2, 0).wait_recv()
            if turn not in DIRECT:
                copy_resid_half(turn, left // 2, 0).start()
            copy_resid(turn, right // 2, 1).wait_recv()
            if turn not in DIRECT:
                copy_resid_half(turn, right // 2, 1).start()

    def await_resid(turn):
        @pl.when(ends_here(pair_at[turn]))
        def _():
            if turn in DIRECT:
                copy_resid_across(turn, 1 - x // 2).wait_recv()
                return
            for side in range(2):
                copy_resid_half(turn, 1 - x // 2, side).wait_recv()

    def step_back(turn, at):
        rows = jnp.concatenate(
            [full[tile_rows(part, pair_at[turn]), :, at].reshape(PART, at.size) for part in range(2)], axis=0
        )
        return jnp.dot(resid[turn], rows, preferred_element_type=f32)

    def accumulate(turns):
        for turn in turns:
            await_resid(turn)

        def add(tile):
            at = pl.ds(pl.multiple_of(tile * TILE, TILE), TILE)
            total = step_back(turns[0], at) if turns[0] == 0 else back[:, at] + step_back(turns[0], at)
            for turn in turns[1:]:
                total += step_back(turn, at)
            back[:, at] = total

        each(0, width // TILE, add)

    inner[...] = jnp.zeros(inner.shape, f32)
    far = NZ // 2
    jobs = {
        4: ((project, 0), None, None, None),
        5: ((project, 1), (relay_sums, 0), None, None),
        6: ((project, 2), (relay_sums, 1), None, (subtract, 0)),
        7: ((project, 3), (relay_sums, 2), (subtract, 1), (relay_resid, 0)),
        8: ((project, 4), (relay_sums, 3), (subtract, 2), (relay_resid, 1)),
        9: ((project, 5), (relay_sums, 4), (subtract, 3), (relay_resid, 2)),
        10: ((project, 6), (relay_sums, 5), (subtract, 4), (relay_resid, 3)),
    }

    def work(job):
        if job is not None:
            job[0](job[1])

    for distance in range(4, far + 3):
        if distance <= far:
            first_hand(distance, -1, distance < far)
            if distance < far:
                first_hand(distance, 1, distance < far - 1)
        if distance == 4:
            for step in (3, -3, 2, -2):
                send_goal(step)
        if distance == 5:
            for step in (1, -1):
                send_goal(step)
        work(jobs[distance][0])
        if distance - 1 <= far:
            planes(distance - 1, -1, distance - 1 < far)
            if distance - 1 < far:
                planes(distance - 1, 1, distance - 1 < far - 1)
        work(jobs[distance][1])
        if distance - 1 <= far:
            later(second_hand, distance - 1)
        work(jobs[distance][2])
        later(third_hand, distance - 2)
        if distance == 6:
            each(1, NZ, lambda step: copy_goalz(z, zz_of(step)).wait_recv())
        work(jobs[distance][3])
    project(7)
    subtract(5)
    relay_resid(4)
    subtract(6)
    accumulate((0, 1))
    relay_resid(5)
    subtract(7)

    inner_row = as_row(jnp.sum(inner[...], axis=1, keepdims=True))
    inner_out[...] = jnp.broadcast_to(inner_row, inner_out.shape)
    for step in range(1, NX):
        copy_inner(step).start()
    accumulate((2, 3, 4, 5))
    relay_resid(6)
    relay_resid(7)
    wanted_row = as_row(wanted)
    wanted_ref[...] = jnp.broadcast_to(wanted_row, wanted_ref.shape)
    for step in range(1, NX):
        copy_inner(step).wait_recv()
    inner_all = inner_row
    for step in range(1, NX):
        inner_all += inner_in[step - 1][0:1, :]
    pull = row_scale * row_scale * as_column(inner_all) / D
    await_resid(6)
    await_resid(7)

    def finish(tile):
        at = pl.ds(pl.multiple_of(tile * TILE, TILE), TILE)
        weighted = (back[:, at] + step_back(6, at) + step_back(7, at)) * gain[:, at]
        grad_ref[:, at] = (row_scale * weighted - hidden[:, at].astype(f32) * pull).astype(bf16)

    each(0, width // TILE, finish)

    def all_sent(ref, sem):
        pltpu.make_async_copy(ref, ref, sem).wait()

    all_sent(full.at[pl.ds(0, GROUP - 1), :, cols_a], sent_a)
    all_sent(full.at[pl.ds(0, GROUP - 1), :, cols_b], sent_b)
    all_sent(ids_out.at[pl.ds(0, spots - 1)], many_sent.at[0])
    all_sent(ids_in.at[pl.ds(0, NZ - 1)], many_sent.at[1])
    all_sent(goal_out.at[pl.ds(0, spots - 1)], many_sent.at[2])
    all_sent(goal_next.at[pl.ds(0, NZ - 1)], many_sent.at[3])
    for step in range(1, NX):
        copy_square(step).wait_send()
        copy_inner(step).wait_send()
    for turn in range(TURNS):
        dest = ends_here(pair_at[turn])

        @pl.when(dest)
        def _():
            if turn in DIRECT:
                copy_direct(turn).wait_send()
                copy_resid_across(turn, x // 2).wait_send()
            for side in range(2):
                if turn not in DIRECT:
                    copy_half(turn, side).wait_send()
                copy_resid(turn, x // 2, side).wait_send()

        @pl.when(jnp.logical_not(dest))
        def _():
            if turn not in DIRECT:
                copy_resid_half(turn, left // 2, 0).wait_send()
                copy_resid_half(turn, right // 2, 1).wait_send()
            for side in range(2):
                copy_joint(turn, side).wait_send()


def put_rows(wanted_ref, grad_ref, out_ref):
    rows = out_ref.shape[0]
    at = lax.broadcasted_iota(jnp.int32, (rows, grad_ref.shape[0]), 0).astype(jnp.float32)
    put = jnp.where(at == wanted_ref[0:1, :], 1.0, 0.0).astype(jnp.bfloat16)
    out_ref[...] = jnp.dot(put, grad_ref[...], preferred_element_type=jnp.float32).astype(out_ref.dtype)


def on_device(token_shard, token_row, table, gain, key_value_weight, kv_target):
    tokens = token_row.shape[0]
    depth, width = key_value_weight.shape
    kept = kv_target.shape[1]
    slots = 2 * tokens
    spots = NY * NC
    bf16, f32, i32 = jnp.bfloat16, jnp.float32, jnp.int32
    dma, vmem = pltpu.SemaphoreType.DMA, pltpu.VMEM
    outside = pl.BlockSpec(memory_space=pltpu.HBM)
    grad, wanted = pl.pallas_call(
        kernel,
        out_shape=(jax.ShapeDtypeStruct((slots, width), bf16), jax.ShapeDtypeStruct((8, slots), f32)),
        in_specs=[outside] * 6,
        out_specs=(pl.BlockSpec(memory_space=vmem),) * 2,
        scratch_shapes=[
            vmem((1, tokens), i32),
            vmem((1, tokens), i32),
            vmem((tokens, kept), bf16),
            vmem((1, width), f32),
            vmem((GROUP, depth, width), bf16),
            vmem(table.shape, bf16),
            vmem((spots, 8, 128), f32),
            vmem((spots, 8, 128), f32),
            vmem((spots, 128), f32),
            vmem((NZ, spots, 128), f32),
            vmem((spots, slots // spots, kept), bf16),
            vmem((spots, slots // spots, kept), bf16),
            vmem((NZ, slots // NZ, kept), bf16),
            vmem((NZ, slots // NZ, kept), bf16),
            vmem((slots, width), bf16),
            vmem((slots, width), bf16),
            vmem((TURNS, slots, 2 * PART), f32),
            vmem((TURNS, 2, HALF, PART), bf16),
            vmem((TURNS, 2, HALF, PART), bf16),
            vmem((TURNS, 2, slots, PART), bf16),
            vmem((TURNS, 2, slots, PART), bf16),
            vmem((len(DIRECT), slots, PART), bf16),
            vmem((len(DIRECT), slots, PART), bf16),
            vmem((TURNS, slots, 2 * PART), bf16),
            vmem((slots, PART), f32),
            vmem((slots, width), f32),
            vmem((8, slots), f32),
            vmem((NX - 1, 8, slots), f32),
            vmem((8, slots), f32),
            vmem((NX - 1, 8, slots), f32),
            dma((6,)),
            dma((GROUP,)),
            dma((GROUP,)),
            dma,
            dma,
            dma((spots,)),
            dma((NZ,)),
            dma((spots,)),
            dma((NZ,)),
            dma((4,)),
            dma((NX - 1,)),
            dma((NX - 1,)),
            dma((NX - 1,)),
            dma((NX - 1,)),
            dma((TURNS, 2)),
            dma((TURNS, 2)),
            dma((TURNS, 2)),
            dma((TURNS, 2)),
            dma((TURNS, 2, 2)),
            dma((TURNS, 2)),
            dma((len(DIRECT),)),
            dma((len(DIRECT),)),
            dma((len(DIRECT),)),
        ],
        compiler_params=pltpu.CompilerParams(
            collective_id=0, has_side_effects=True, vmem_limit_bytes=59936 * 1024
        ),
    )(
        token_shard.reshape(1, tokens),
        token_row.reshape(1, tokens),
        kv_target,
        gain.reshape(1, width),
        key_value_weight,
        table,
    )
    step = width // 2
    return pl.pallas_call(
        put_rows,
        out_shape=jax.ShapeDtypeStruct(table.shape, bf16),
        grid=(width // step,),
        in_specs=[
            pl.BlockSpec((8, slots), lambda tile: (0, 0)),
            pl.BlockSpec((slots, step), lambda tile: (0, tile)),
        ],
        out_specs=pl.BlockSpec((table.shape[0], step), lambda tile: (0, tile)),
    )(wanted, grad)


def solution(mesh):
    return jax.shard_map(
        on_device,
        mesh=mesh,
        in_specs=(
            P(("section", "wide"), None),
            P(("section", "wide")),
            P(("section", "wide"), "narrow"),
            P("narrow"),
            P(("section", "wide"), "narrow"),
            P(("section", "wide"), "narrow"),
        ),
        out_specs=P(("section", "wide"), "narrow"),
        check_vma=False,
    )
```

```python
import functools

import jax
import jax.numpy as jnp
from jax import lax
from jax.experimental import pallas as pl
from jax.experimental.pallas import tpu as pltpu
from jax.sharding import PartitionSpec as P

MESH = pl.DeviceIdType.MESH
D = 8192
EPSILON = 1e-05
NY, NZ, NC, NX = 4, 16, 2, 4
GROUP = NY * NZ * NC
SPLIT = 512
TILE = 256
PART = 128
DIRECT = (6, 7)
HALF = 128
TURNS = 8


def kernel(
    shard_hbm,
    row_hbm,
    target_hbm,
    gain_hbm,
    weight_hbm,
    table_hbm,
    grad_ref,
    wanted_ref,
    shard,
    row,
    target,
    gain,
    full,
    table,
    ids_out,
    ids_mid,
    ids_all,
    ids_in,
    goal_out,
    goal_mid,
    goal_next,
    goal,
    hidden,
    normed,
    partial,
    half_out,
    half_in,
    joint_out,
    joint_in,
    direct_out,
    direct_in,
    resid,
    inner,
    back,
    square_out,
    square_in,
    inner_out,
    inner_in,
    local_sem,
    recv_a,
    recv_b,
    sent_a,
    sent_b,
    idy_recv,
    idz_recv,
    goaly_recv,
    goalz_recv,
    many_sent,
    square_recv,
    square_sent,
    inner_recv,
    inner_sent,
    half_recv,
    half_sent,
    joint_recv,
    joint_sent,
    resid_recv,
    resid_sent,
    direct_recv,
    direct_sent,
    across_sent,
    entered,
):
    f32, bf16, i32 = jnp.float32, jnp.bfloat16, jnp.int32
    section, wide, x = lax.axis_index("section"), lax.axis_index("wide"), lax.axis_index("narrow")
    z, c = wide // 4, wide % 2
    y = section * 2 + (wide // 2) % 2
    here = y * 2 + c
    tokens, kept = target.shape
    slots = normed.shape[0]
    depth, width = full.shape[1:]
    rows_here = table.shape[0]
    cols_a, cols_b = pl.ds(0, SPLIT), pl.ds(SPLIT, width - SPLIT)
    spots = NY * NC
    per_y, per_z = slots // spots, slots // NZ

    def device(yy, zz, cc, xx):
        return (yy // 2, zz * 4 + (yy % 2) * 2 + cc, xx)

    def block(yy, zz, cc):
        return (yy // 2) * (NZ * 4) + zz * 4 + (yy % 2) * 2 + cc

    def yy_of(step):
        return lax.rem(y + step + NY, NY)

    def zz_of(step):
        return lax.rem(z + step + NZ, NZ)

    def xx_of(step):
        return lax.rem(x + step + NX, NX)

    def beside(xx):
        return device(y, z, c, xx)

    def remote(source, landing, sent, recv, to):
        return pltpu.make_async_remote_copy(
            src_ref=source, dst_ref=landing, send_sem=sent, recv_sem=recv, device_id=to, device_id_type=MESH
        )

    loads = [
        pltpu.make_async_copy(source, landing, local_sem.at[number])
        for number, (source, landing) in enumerate(
            (
                (shard_hbm, shard),
                (row_hbm, row),
                (weight_hbm, full.at[block(y, z, c)]),
                (target_hbm, target),
                (gain_hbm, gain),
                (table_hbm, table),
            )
        )
    ]
    for load in loads:
        load.start()

    barrier = pltpu.get_barrier_semaphore()

    for step in (1, -1):
        pl.semaphore_signal(barrier, inc=1, device_id=device(y, zz_of(step), c, x), device_id_type=MESH)

    def greet_y(step, carry):
        other = lax.rem(here + step, spots)
        pl.semaphore_signal(barrier, inc=1, device_id=device(other // 2, z, other % 2, x), device_id_type=MESH)
        return carry

    lax.fori_loop(1, spots, greet_y, 0)
    for step in range(1, NX):
        pl.semaphore_signal(barrier, inc=1, device_id=beside(xx_of(step)), device_id_type=MESH)

    loads[0].wait()
    loads[1].wait()
    first = lax.broadcasted_iota(i32, (tokens, tokens), 0)
    second = lax.broadcasted_iota(i32, (tokens, tokens), 1)
    holder = shard[...]
    holder_col = jnp.sum(jnp.where(first == second, holder, 0), axis=1, keepdims=True)
    same = jnp.logical_and(holder_col == holder, first < second)
    rank = jnp.sum(jnp.where(same, 1, 0), axis=0, keepdims=True)
    hold_z = (holder // 4) % NZ
    hold_y = (holder // 64) * 4 + holder % 4
    slot_of = hold_y * per_y + hold_z * 2 + rank
    placed = lax.broadcasted_iota(i32, (slots, tokens), 0) == slot_of
    slot_id = jnp.sum(jnp.where(placed, row[...] + 1, 0), axis=1, keepdims=True).astype(f32)
    spread_ids = lax.broadcasted_iota(i32, (per_y, 128), 0) == lax.broadcasted_iota(i32, (per_y, 128), 1)
    for spot in range(spots):
        line = jnp.sum(
            jnp.where(spread_ids, slot_id[spot * per_y : (spot + 1) * per_y], 0.0), axis=0, keepdims=True
        )
        ids_out[spot] = jnp.broadcast_to(line, (8, 128))
    loads[3].wait()
    place = jnp.where(placed, 1.0, 0.0).astype(bf16)
    goal_out[...] = (
        jnp.dot(place, target[...], preferred_element_type=f32).astype(bf16).reshape(spots, per_y, kept)
    )
    loads[2].wait()

    pl.semaphore_wait(barrier, 2 + (spots - 1) + (NX - 1))

    def tell(side, distance):
        to = device(y, zz_of(-1 if side else 1), c, x)
        pl.semaphore_signal(entered.at[side, distance], inc=1, device_id=to, device_id_type=MESH)

    def learn(distance):
        for side in range(2):
            last = NZ // 2 - side
            if distance <= last:
                pl.semaphore_wait(entered.at[side, distance], 1)
                if distance < last:
                    tell(side, distance + 1)

    tell(0, 2)
    tell(1, 2)

    def spot_device(spot):
        return device(spot // 2, z, spot % 2, x)

    def copy_idy(to, source):
        return remote(ids_out.at[to], ids_mid.at[source], many_sent.at[0], idy_recv.at[source], spot_device(to))

    def copy_idz(to, source):
        return remote(ids_all, ids_in.at[source], many_sent.at[1], idz_recv.at[source], device(y, to, c, x))

    def copy_goaly(to, source):
        return remote(goal_out.at[to], goal_mid.at[source], many_sent.at[2], goaly_recv.at[source], spot_device(to))

    def copy_goalz(to, source):
        return remote(goal_next.at[to], goal.at[source], many_sent.at[3], goalz_recv.at[source], device(y, to, c, x))

    def copy_weight(which, yy, zz, cc, to):
        cols, recv, sent = (cols_a, recv_a, sent_a) if which == "a" else (cols_b, recv_b, sent_b)
        piece = full.at[block(yy, zz, cc), :, cols]
        return remote(piece, piece, sent, recv.at[block(yy, zz, cc)], to)

    above, below = device(yy_of(1), z, c, x), device(yy_of(-1), z, c, x)
    opposite = device(yy_of(2), z, c, x)
    after, before = device(y, zz_of(1), c, x), device(y, zz_of(-1), c, x)
    partner = device(y, z, 1 - c, x)

    def pass_on(which, yy, zz, targets):
        for to in targets:
            copy_weight(which, yy, zz, c, to).start()

    def arrive(which, yy, zz, cc):
        copy_weight(which, yy, zz, cc, partner).wait_recv()

    def each(low, high, act):
        def step(index, carry):
            act(index)
            return carry

        lax.fori_loop(low, high, step, 0)

    def around(step):
        return lax.rem(here + step, spots)

    pass_on("b", y, z, (after, before))
    pass_on("a", y, z, (above, below, opposite))
    each(1, spots, lambda step: copy_idy(around(step), here).start())
    each(1, spots, lambda step: copy_goaly(around(step), here).start())
    pass_on("b", y, z, (above, below))
    pass_on("a", y, z, (after, before, partner))
    pass_on("b", y, z, (partner,))
    ids_mid[here] = ids_out[here]
    goal_mid[here] = goal_out[here]

    def when(condition, act):
        if isinstance(condition, bool):
            if condition:
                act()
        else:
            pl.when(condition)(act)

    def onward(which, yy, zz, sign, ahead):
        to = after if sign < 0 else before
        when(ahead, lambda: pass_on(which, yy, zz, (to,)))

    def first_hand(distance, sign, ahead):
        zz = zz_of(sign * distance)
        arrive("b", y, zz, c)
        onward("b", y, zz, sign, ahead)
        pass_on("b", y, zz, (above, below, partner))

    def planes(distance, sign, ahead):
        zz = zz_of(sign * distance)
        for step in range(NY):
            arrive("a", yy_of(step), zz, c)
            onward("a", yy_of(step), zz, sign, ahead)
            pass_on("a", yy_of(step), zz, (partner,))

    def second_hand(distance, sign):
        zz = zz_of(sign * distance)
        arrive("b", yy_of(-1), zz, c)
        when(distance % 2 == 0, lambda: pass_on("b", yy_of(-1), zz, (above,)))
        pass_on("b", yy_of(-1), zz, (partner,))
        arrive("b", yy_of(1), zz, c)
        when(distance % 2 == 1, lambda: pass_on("b", yy_of(1), zz, (below,)))
        pass_on("b", yy_of(1), zz, (partner,))

    def third_hand(distance, sign):
        zz = zz_of(sign * distance)
        arrive("b", yy_of(2), zz, c)
        pass_on("b", yy_of(2), zz, (partner,))

    def later(hand, distance):
        if isinstance(distance, int):
            if distance >= 0:
                hand(distance, -1)
            if 1 <= distance < NZ // 2:
                hand(distance, 1)
            return
        pl.when(distance >= 0)(lambda: hand(distance, -1))
        pl.when(distance >= 1)(lambda: hand(distance, 1))

    def send_goal(step):
        copy_goalz(zz_of(step), z).start()

    def both(hand, distance):
        hand(distance, -1, True)
        hand(distance, 1, True)

    learn(2)
    learn(3)
    both(first_hand, 1)
    learn(4)
    learn(5)
    for step in range(1, NY):
        arrive("a", yy_of(step), z, c)
        pass_on("a", yy_of(step), z, (after, before, partner))
    learn(6)
    both(first_hand, 2)
    learn(7)
    learn(8)
    each(1, spots, lambda step: copy_idy(here, around(step)).wait_recv())
    ids_all[...] = jnp.concatenate([ids_mid[spot][0:1, :] for spot in range(spots)], axis=0)
    each(1, NZ, lambda step: copy_idz(zz_of(step), z).start())
    ids_in[z] = ids_all[...]
    both(planes, 1)
    later(second_hand, 0)

    each(1, spots, lambda step: copy_goaly(here, around(step)).wait_recv())
    out_slot = lax.broadcasted_iota(i32, (slots, slots), 0)
    in_slot = lax.broadcasted_iota(i32, (slots, slots), 1)
    inside = out_slot % per_z
    from_slot = (inside % spots) * per_y + (out_slot // per_z) * 2 + inside // spots
    order = jnp.where(in_slot == from_slot, 1.0, 0.0).astype(bf16)
    arrived = goal_mid[...].reshape(slots, kept)
    goal_next[...] = jnp.dot(order, arrived, preferred_element_type=f32).astype(bf16).reshape(NZ, per_z, kept)
    send_goal(8)
    goal[z] = goal_next[z]

    both(first_hand, 3)
    for step in (7, -7, 1, -1):
        send_goal(step)
    both(planes, 2)
    later(second_hand, 1)
    later(third_hand, 0)

    each(1, NZ, lambda step: copy_idz(z, zz_of(step)).wait_recv())
    loads[5].wait()
    loads[4].wait()
    listed = ids_in[...].reshape(NZ * spots, 128)
    lane = lax.broadcasted_iota(i32, listed.shape, 1)
    wanted = (
        jnp.concatenate(
            [
                jnp.sum(jnp.where(lane == 2 * z + k, listed, 0.0), axis=1, keepdims=True).reshape(NZ, spots, 1)
                for k in range(2)
            ],
            axis=1,
        ).reshape(slots, 1)
        - 1.0
    )
    pick = jnp.where(lax.broadcasted_iota(i32, (slots, rows_here), 1).astype(f32) == wanted, 1.0, 0.0).astype(bf16)
    square_sum = jnp.zeros((slots, 1), f32)
    for tile in range(width // 512):
        at = pl.ds(tile * 512, 512)
        picked = jnp.dot(pick, table[:, at], preferred_element_type=f32)
        hidden[:, at] = picked.astype(bf16)
        square_sum += jnp.sum(picked * picked, axis=1, keepdims=True)
    diagonal = out_slot == in_slot

    def as_row(column):
        return jnp.sum(jnp.where(diagonal, column, 0.0), axis=0, keepdims=True)

    def as_column(line):
        return jnp.sum(jnp.where(diagonal, line, 0.0), axis=1, keepdims=True)

    def copy_square(step):
        return remote(
            square_out, square_in.at[step - 1], square_sent.at[step - 1], square_recv.at[step - 1], beside(xx_of(step))
        )

    def copy_inner(step):
        return remote(
            inner_out, inner_in.at[step - 1], inner_sent.at[step - 1], inner_recv.at[step - 1], beside(xx_of(step))
        )

    square_row = as_row(square_sum)
    square_out[...] = jnp.broadcast_to(square_row, square_out.shape)
    for step in range(1, NX):
        copy_square(step).start()

    later(second_hand, 2)
    later(third_hand, 1)

    for step in range(1, NX):
        copy_square(step).wait_recv()
    total = square_row
    for step in range(1, NX):
        total += square_in[step - 1][0:1, :]
    row_scale = lax.rsqrt(as_column(total) / D + EPSILON)
    for tile in range(width // 512):
        at = pl.ds(tile * 512, 512)
        normed[:, at] = (hidden[:, at].astype(f32) * row_scale * gain[:, at]).astype(bf16)

    pairs = NZ // 2
    mine, lean = z // 2, 1 - 2 * (z % 2)
    pair_at = [
        lax.rem(mine + lean * (-((turn + 1) // 2) if turn % 2 else turn // 2) + pairs, pairs) for turn in range(TURNS)
    ]
    blocks = PART // depth
    right, left = xx_of(1), xx_of(-1)

    def copy_direct(turn):
        at = turn - DIRECT[0]
        return remote(direct_out.at[at], direct_in.at[at], direct_sent.at[at], direct_recv.at[at], beside(xx_of(2)))

    def copy_resid_across(turn, part):
        piece = resid.at[turn, :, part_cols(part)]
        return remote(
            piece, piece, across_sent.at[turn - DIRECT[0]], resid_recv.at[turn, part, 0], beside(xx_of(2))
        )

    def tile_rows(part, pair):
        return pl.ds((part * pairs + pair) * blocks, blocks)

    def ends_here(pair):
        return x % 2 == pair // (pairs // 2)

    def copy_half(turn, side):
        return remote(
            half_out.at[turn, side],
            half_in.at[turn, side],
            half_sent.at[turn, side],
            half_recv.at[turn, side],
            beside(left if side else right),
        )

    def copy_joint(turn, side):
        return remote(
            joint_out.at[turn, side],
            joint_in.at[turn, side],
            joint_sent.at[turn, side],
            joint_recv.at[turn, side],
            beside(left if side else right),
        )

    def part_cols(part):
        return pl.ds(pl.multiple_of(part * PART, PART), PART)

    def side_rows(side):
        return pl.ds(side * HALF, HALF)

    def copy_resid(turn, part, side):
        piece = resid.at[turn, :, part_cols(part)]
        return remote(
            piece, piece, resid_sent.at[turn, side], resid_recv.at[turn, part, 0], beside(left if side else right)
        )

    def copy_resid_half(turn, part, side):
        piece = resid.at[turn, side_rows(side), part_cols(part)]
        return remote(
            piece, piece, resid_sent.at[turn, side], resid_recv.at[turn, part, side], beside(left if side else right)
        )

    def project(turn):
        pair = pair_at[turn]
        for step in range(2):
            for yy in range(NY):
                arrive("a", yy, pair * 2 + step, 1 - c)
                arrive("b", yy, pair * 2 + step, 1 - c)
        dest = ends_here(pair)
        order = (jnp.where(dest, 1 - x // 2, right // 2), jnp.where(dest, x // 2, left // 2))
        rows = jnp.concatenate([full[tile_rows(part, pair)].reshape(PART, width) for part in order], axis=0)
        partial[turn] = lax.dot_general(normed[...], rows, (((1,), (1,)), ((), ())), preferred_element_type=f32)

        if turn in DIRECT:

            @pl.when(dest)
            def _():
                direct_out[turn - DIRECT[0]] = partial[turn, :, 0:PART].astype(bf16)
                copy_direct(turn).start()

            @pl.when(jnp.logical_not(dest))
            def _():
                for side in range(2):
                    joint_out[turn, side] = partial[turn, :, side * PART : (side + 1) * PART].astype(bf16)
                    copy_joint(turn, side).start()

            return

        @pl.when(dest)
        def _():
            for side in range(2):
                half_out[turn, side] = partial[turn, side_rows(side), 0:PART].astype(bf16)
                copy_half(turn, side).start()

    def relay_sums(turn):
        @pl.when(jnp.logical_not(ends_here(pair_at[turn])))
        def _():
            for side in range(2):
                copy_half(turn, side).wait_recv()
                near, far, at = side_rows(side), side_rows(1 - side), slice(side * PART, (side + 1) * PART)
                joint_out[turn, side, near] = (partial[turn, near, at] + half_in[turn, side].astype(f32)).astype(bf16)
                joint_out[turn, side, far] = partial[turn, far, at].astype(bf16)
                copy_joint(turn, side).start()

    def subtract(turn):
        pair = pair_at[turn]

        @pl.when(ends_here(pair))
        def _():
            for side in range(2):
                copy_joint(turn, side).wait_recv()
            projected = partial[turn, :, PART:] + joint_in[turn, 0].astype(f32) + joint_in[turn, 1].astype(f32)
            if turn in DIRECT:
                copy_direct(turn).wait_recv()
                projected += direct_in[turn - DIRECT[0]].astype(f32)
            wished = goal[:, :, part_cols(pair % (pairs // 2))].reshape(slots, PART)
            residual = (projected - wished.astype(f32)).astype(bf16)
            resid[turn, :, part_cols(x // 2)] = residual
            for side in range(2):
                copy_resid(turn, x // 2, side).start()
            if turn in DIRECT:
                copy_resid_across(turn, x // 2).start()
            inner[...] += projected * residual.astype(f32)

    def relay_resid(turn):
        @pl.when(jnp.logical_not(ends_here(pair_at[turn])))
        def _():
            copy_resid(turn, left // 2, 0).wait_recv()
            if turn not in DIRECT:
                copy_resid_half(turn, left // 2, 0).start()
            copy_resid(turn, right // 2, 1).wait_recv()
            if turn not in DIRECT:
                copy_resid_half(turn, right // 2, 1).start()

    def await_resid(turn):
        @pl.when(ends_here(pair_at[turn]))
        def _():
            if turn in DIRECT:
                copy_resid_across(turn, 1 - x // 2).wait_recv()
                return
            for side in range(2):
                copy_resid_half(turn, 1 - x // 2, side).wait_recv()

    def step_back(turn, at):
        rows = jnp.concatenate(
            [full[tile_rows(part, pair_at[turn]), :, at].reshape(PART, at.size) for part in range(2)], axis=0
        )
        return jnp.dot(resid[turn], rows, preferred_element_type=f32)

    def accumulate(turns):
        for turn in turns:
            await_resid(turn)

        def add(tile):
            at = pl.ds(pl.multiple_of(tile * TILE, TILE), TILE)
            total = step_back(turns[0], at) if turns[0] == 0 else back[:, at] + step_back(turns[0], at)
            for turn in turns[1:]:
                total += step_back(turn, at)
            back[:, at] = total

        each(0, width // TILE, add)

    inner[...] = jnp.zeros(inner.shape, f32)
    def relay_both(turn):
        relay_resid(turn)
        relay_resid(turn + 1)

    far = NZ // 2
    jobs = {
        4: ((project, 0), None, None, None),
        5: ((project, 1), (relay_sums, 0), None, None),
        6: ((project, 2), (relay_sums, 1), None, None),
        7: ((project, 3), (relay_sums, 2), (subtract, 0), (subtract, 1)),
        8: ((project, 4), (relay_sums, 3), (subtract, 2), (relay_both, 0)),
        9: ((project, 5), (relay_sums, 4), (subtract, 3), (relay_resid, 2)),
        10: ((project, 6), (relay_sums, 5), (subtract, 4), (relay_resid, 3)),
    }

    def work(job):
        if job is not None:
            job[0](job[1])

    for distance in range(4, far + 3):
        if distance <= far:
            first_hand(distance, -1, distance < far)
            if distance < far:
                first_hand(distance, 1, distance < far - 1)
        for step in {4: (6, -6, 2, -2), 5: (5, -5, 3, -3), 6: (4, -4)}.get(distance, ()):
            send_goal(step)
        work(jobs[distance][0])
        if distance - 1 <= far:
            planes(distance - 1, -1, distance - 1 < far)
            if distance - 1 < far:
                planes(distance - 1, 1, distance - 1 < far - 1)
        work(jobs[distance][1])
        if distance - 1 <= far:
            later(second_hand, distance - 1)
        if distance == 7:
            each(1, NZ, lambda step: copy_goalz(z, zz_of(step)).wait_recv())
        work(jobs[distance][2])
        later(third_hand, distance - 2)
        work(jobs[distance][3])
    project(7)
    subtract(5)
    relay_resid(4)
    subtract(6)
    accumulate((0, 1))
    relay_resid(5)
    subtract(7)

    inner_row = as_row(jnp.sum(inner[...], axis=1, keepdims=True))
    inner_out[...] = jnp.broadcast_to(inner_row, inner_out.shape)
    for step in range(1, NX):
        copy_inner(step).start()
    accumulate((2, 3, 4, 5))
    relay_resid(6)
    relay_resid(7)
    wanted_row = as_row(wanted)
    wanted_ref[...] = jnp.broadcast_to(wanted_row, wanted_ref.shape)
    for step in range(1, NX):
        copy_inner(step).wait_recv()
    inner_all = inner_row
    for step in range(1, NX):
        inner_all += inner_in[step - 1][0:1, :]
    pull = row_scale * row_scale * as_column(inner_all) / D
    await_resid(6)
    await_resid(7)

    def finish(tile):
        at = pl.ds(pl.multiple_of(tile * TILE, TILE), TILE)
        weighted = (back[:, at] + step_back(6, at) + step_back(7, at)) * gain[:, at]
        grad_ref[:, at] = (row_scale * weighted - hidden[:, at].astype(f32) * pull).astype(bf16)

    each(0, width // TILE, finish)

    def all_sent(ref, sem):
        pltpu.make_async_copy(ref, ref, sem).wait()

    all_sent(full.at[pl.ds(0, GROUP - 1), :, cols_a], sent_a)
    all_sent(full.at[pl.ds(0, GROUP - 1), :, cols_b], sent_b)
    all_sent(ids_out.at[pl.ds(0, spots - 1)], many_sent.at[0])
    all_sent(ids_in.at[pl.ds(0, NZ - 1)], many_sent.at[1])
    all_sent(goal_out.at[pl.ds(0, spots - 1)], many_sent.at[2])
    all_sent(goal_next.at[pl.ds(0, NZ - 1)], many_sent.at[3])
    for step in range(1, NX):
        copy_square(step).wait_send()
        copy_inner(step).wait_send()
    for turn in range(TURNS):
        dest = ends_here(pair_at[turn])

        @pl.when(dest)
        def _():
            if turn in DIRECT:
                copy_direct(turn).wait_send()
                copy_resid_across(turn, x // 2).wait_send()
            for side in range(2):
                if turn not in DIRECT:
                    copy_half(turn, side).wait_send()
                copy_resid(turn, x // 2, side).wait_send()

        @pl.when(jnp.logical_not(dest))
        def _():
            if turn not in DIRECT:
                copy_resid_half(turn, left // 2, 0).wait_send()
                copy_resid_half(turn, right // 2, 1).wait_send()
            for side in range(2):
                copy_joint(turn, side).wait_send()


def put_rows(wanted_ref, grad_ref, out_ref):
    rows = out_ref.shape[0]
    at = lax.broadcasted_iota(jnp.int32, (rows, grad_ref.shape[0]), 0).astype(jnp.float32)
    put = jnp.where(at == wanted_ref[0:1, :], 1.0, 0.0).astype(jnp.bfloat16)
    out_ref[...] = jnp.dot(put, grad_ref[...], preferred_element_type=jnp.float32).astype(out_ref.dtype)


def on_device(token_shard, token_row, table, gain, key_value_weight, kv_target):
    tokens = token_row.shape[0]
    depth, width = key_value_weight.shape
    kept = kv_target.shape[1]
    slots = 2 * tokens
    spots = NY * NC
    bf16, f32, i32 = jnp.bfloat16, jnp.float32, jnp.int32
    dma, vmem = pltpu.SemaphoreType.DMA, pltpu.VMEM
    outside = pl.BlockSpec(memory_space=pltpu.HBM)
    grad, wanted = pl.pallas_call(
        kernel,
        out_shape=(jax.ShapeDtypeStruct((slots, width), bf16), jax.ShapeDtypeStruct((8, slots), f32)),
        in_specs=[outside] * 6,
        out_specs=(pl.BlockSpec(memory_space=vmem),) * 2,
        scratch_shapes=[
            vmem((1, tokens), i32),
            vmem((1, tokens), i32),
            vmem((tokens, kept), bf16),
            vmem((1, width), f32),
            vmem((GROUP, depth, width), bf16),
            vmem(table.shape, bf16),
            vmem((spots, 8, 128), f32),
            vmem((spots, 8, 128), f32),
            vmem((spots, 128), f32),
            vmem((NZ, spots, 128), f32),
            vmem((spots, slots // spots, kept), bf16),
            vmem((spots, slots // spots, kept), bf16),
            vmem((NZ, slots // NZ, kept), bf16),
            vmem((NZ, slots // NZ, kept), bf16),
            vmem((slots, width), bf16),
            vmem((slots, width), bf16),
            vmem((TURNS, slots, 2 * PART), f32),
            vmem((TURNS, 2, HALF, PART), bf16),
            vmem((TURNS, 2, HALF, PART), bf16),
            vmem((TURNS, 2, slots, PART), bf16),
            vmem((TURNS, 2, slots, PART), bf16),
            vmem((len(DIRECT), slots, PART), bf16),
            vmem((len(DIRECT), slots, PART), bf16),
            vmem((TURNS, slots, 2 * PART), bf16),
            vmem((slots, PART), f32),
            vmem((slots, width), f32),
            vmem((8, slots), f32),
            vmem((NX - 1, 8, slots), f32),
            vmem((8, slots), f32),
            vmem((NX - 1, 8, slots), f32),
            dma((6,)),
            dma((GROUP,)),
            dma((GROUP,)),
            dma,
            dma,
            dma((spots,)),
            dma((NZ,)),
            dma((spots,)),
            dma((NZ,)),
            dma((4,)),
            dma((NX - 1,)),
            dma((NX - 1,)),
            dma((NX - 1,)),
            dma((NX - 1,)),
            dma((TURNS, 2)),
            dma((TURNS, 2)),
            dma((TURNS, 2)),
            dma((TURNS, 2)),
            dma((TURNS, 2, 2)),
            dma((TURNS, 2)),
            dma((len(DIRECT),)),
            dma((len(DIRECT),)),
            dma((len(DIRECT),)),
            pltpu.SemaphoreType.REGULAR((2, NZ // 2 + 1)),
        ],
        compiler_params=pltpu.CompilerParams(
            collective_id=0, has_side_effects=True, vmem_limit_bytes=59936 * 1024
        ),
    )(
        token_shard.reshape(1, tokens),
        token_row.reshape(1, tokens),
        kv_target,
        gain.reshape(1, width),
        key_value_weight,
        table,
    )
    step = width // 2
    return pl.pallas_call(
        put_rows,
        out_shape=jax.ShapeDtypeStruct(table.shape, bf16),
        grid=(width // step,),
        in_specs=[
            pl.BlockSpec((8, slots), lambda tile: (0, 0)),
            pl.BlockSpec((slots, step), lambda tile: (0, tile)),
        ],
        out_specs=pl.BlockSpec((table.shape[0], step), lambda tile: (0, tile)),
    )(wanted, grad)


def solution(mesh):
    return jax.shard_map(
        on_device,
        mesh=mesh,
        in_specs=(
            P(("section", "wide"), None),
            P(("section", "wide")),
            P(("section", "wide"), "narrow"),
            P("narrow"),
            P(("section", "wide"), "narrow"),
            P(("section", "wide"), "narrow"),
        ),
        out_specs=P(("section", "wide"), "narrow"),
        check_vma=False,
    )
```
